256 devices in a mesh: shard: 8 (over z_lo, x), tensor: 4 (over z_hi), section: 8 (over y, core).
Axes of the slice: x: 4, y: 4, z: 8 (z_hi: 4, z_lo: 2; z = z_hi * 2 + z_lo), core: 2. Of those that a mesh axis runs over, the one named last changes fastest.
Arguments:
- activations: bfloat16 [8, 2048, 2304], P(None, 'shard', ('tensor', 'section')), may hold values from -6 to 6
- router_grad: bfloat16 [8, 2048], P(None, 'shard'), may hold values from -6 to 6
- token_ids: int32 [2048], P('shard'), may hold values from 0 to 8191
- norm_terms: bfloat16 [2, 2048, 2304], P(None, 'shard', ('tensor', 'section'))
- old_factors: float32 [8, 2304, 2304], P('shard', 'tensor', 'section'), as said below
- old_router_factor: float32 [8, 8], replicated, as said below
- old_norm_diag: float32 [2, 2304], P(None, ('tensor', 'section')), may hold values from 0.5 to 5
- old_embed_diag: float32 [8192], P('tensor'), may hold values from 0.05 to 0.5
Outputs:
- precond_attn: float32 [4, 2304, 2304], P(None, 'tensor', 'section')
- precond_router: float32 [8, 2304], P(None, 'tensor')
- precond_norms: float32 [2, 2304], P(None, ('tensor', 'section'))
- precond_embed: float32 [8192, 2304], P('tensor', 'section')
The draws below stay inside these ranges and needn't reach their ends.
Inputs may be any that keep to these rules, and one draw needn't show every extreme that they name: `old_factors`: each matrix is symmetric with a positive diagonal. `old_router_factor`: symmetric with a positive diagonal.
All inputs are finite; a program needn't handle non-finite values.
Results may differ from the reference program's by a relative error of at most 0.0083.
Values may be sent and summed in bfloat16 or wider, within the bound.
A program may use at most 64 MiB of HBM per device.

```python
import math
import jax
import jax.numpy as jnp
import numpy as np
from jax import lax

D = 2304
EXPERTS = 8
VOCAB = 8192
NFAC = 8
TOK_DEV = 256
TOKENS = 2048


def symmetric_factors(key, count, width):
    key_diag, key_off = jax.random.split(key)
    index = jnp.arange(width, dtype=jnp.float32)
    ramp = 1.0 + 2.0 * index / max(width - 1, 1)
    diag = jnp.exp(jax.random.uniform(key_diag, (count, width), jnp.float32, math.log(0.5), math.log(2.0))) * ramp
    raw = jnp.clip(jax.random.normal(key_off, (count, width, width), jnp.float32), -3.0, 3.0)
    paired = 0.5 * (raw + jnp.swapaxes(raw, 1, 2))
    root = jnp.sqrt(diag)
    offdiag = paired * (0.4 / math.sqrt(width)) * root[:, :, None] * root[:, None, :]
    identity = jnp.eye(width, dtype=jnp.float32)
    return offdiag * (1.0 - identity) + diag[:, :, None] * identity


def draw_old_factors(key, part):
    return symmetric_factors(jax.random.fold_in(key, 11), NFAC, D)


def draw_old_router_factor(key, part):
    return symmetric_factors(jax.random.fold_in(key, 12), 1, EXPERTS)[0]


def draw_norm_terms(key, part):
    inner = jax.random.fold_in(key, 13)
    blocks = TOKENS // TOK_DEV
    rows = (jnp.arange(TOKENS, dtype=jnp.int32) // TOK_DEV).astype(jnp.float32)
    ramp = 1.0 + 2.0 * rows / max(blocks - 1, 1)
    base = jnp.clip(jax.random.normal(inner, (2, TOKENS, D), jnp.float32), -5.0, 5.0)
    return (0.3 * base * ramp[None, :, None]).astype(jnp.bfloat16)


def touch_ends(values, rng, smallest, top_value):
    longest = values.shape.index(max(values.shape))
    spots = []
    for shift in (0, 1):
        where = [jax.random.randint(jax.random.fold_in(rng, axis), (), 0, length) for axis, length in enumerate(values.shape)]
        where[longest] = (where[longest] + shift) % values.shape[longest]
        spots.append(tuple(where))
    return values.at[spots[0]].set(smallest).at[spots[1]].set(top_value)


def block_levels(rng, shape, shards, low, largest):
    loudness = 1.0
    for dim, blocks in shards:
        draws = jax.random.uniform(jax.random.fold_in(jax.random.fold_in(rng, 6), dim), (blocks,), jnp.float32, low / len(shards), largest / len(shards))
        loudness = loudness * jnp.repeat(jnp.exp(draws), shape[dim] // blocks).reshape((-1,) + (1,) * (len(shape) - 1 - dim))
    return loudness


def rank_table(amount, lean):
    loads = [(1 << 20) // math.isqrt(rank ** lean) + 1 for rank in range(1, amount + 1)]
    scale = 1 + sum(loads) // (1 << 30)
    return np.cumsum(np.array([max(1, weight // scale) for weight in loads]))


def ranked(own_key, dims, number_of, lean):
    grid = rank_table(number_of, lean)
    ticket = jax.random.randint(jax.random.fold_in(own_key, 1), dims, 0, int(grid[number_of - 1]))
    rank = jnp.searchsorted(jnp.asarray(grid, jnp.int32), ticket, side="right")
    return jax.random.permutation(jax.random.fold_in(own_key, 2), number_of)[rank].astype(jnp.int32)


def centred(stream_key, shape, scale, limit, shards=(), kind=jnp.bfloat16):
    entries = scale * jax.random.normal(stream_key, shape, jnp.float32)
    if shards:
        entries = entries * block_levels(stream_key, shape, shards, -0.22, 0.18)
    return jnp.clip(entries, -limit, limit).astype(kind)


def setup_inputs(seed: int = 0) -> dict:
    splits = jax.random.split(jax.random.key(seed), 9)
    activations = centred(splits[0], (NFAC, TOKENS, D), 1.0, 6.0, ((1, 8), (2, 32)))
    router_grad = centred(splits[1], (EXPERTS, TOKENS), 1.0, 6.0, ((1, 8),))
    token_ids = touch_ends(ranked(splits[2], (TOKENS,), VOCAB, 2), jax.random.fold_in(splits[2], 3), 0, VOCAB - 1).astype(jnp.int32)
    norm_terms = draw_norm_terms(jax.random.fold_in(splits[8], 71), 0)
    old_factors = draw_old_factors(jax.random.fold_in(splits[8], 71), 0)
    old_router_factor = draw_old_router_factor(jax.random.fold_in(splits[8], 71), 0)
    old_norm_diag = jnp.clip(jnp.exp(math.log(5.0) - 2.3025851 * jax.random.uniform(splits[6], (2, D), jnp.float32) ** block_levels(splits[6], (2, D), ((1, 32),), -0.2, 0.2)), 0.5, 5.0)
    old_embed_diag = jnp.clip(jnp.exp(math.log(0.5) - 2.3025851 * jax.random.uniform(splits[7], (VOCAB,), jnp.float32) ** block_levels(splits[7], (VOCAB,), ((0, 4),), -0.2, 0.2)), 0.05, 0.5)
    return {"activations": activations, "router_grad": router_grad, "token_ids": token_ids, "norm_terms": norm_terms, "old_factors": old_factors, "old_router_factor": old_router_factor, "old_norm_diag": old_norm_diag, "old_embed_diag": old_embed_diag}


factor_decay = 0.5
damping = 0.01
learning_rate = 0.05


def newton_schulz(matrix):
    width = matrix.shape[0]
    trace = jnp.sum(jnp.diagonal(matrix))
    factor_scale = width / (3.0 * trace)
    identity = jnp.eye(width, dtype=jnp.float32)
    matrix_low = lax.optimization_barrier(matrix.astype(jnp.bfloat16))
    first = 2.0 * factor_scale * identity - factor_scale * factor_scale * matrix_low.astype(jnp.float32)
    first_low = first.astype(jnp.bfloat16)
    image = jnp.dot(matrix_low, first_low, preferred_element_type=jnp.float32).astype(jnp.bfloat16)
    product = jnp.dot(first_low, image, preferred_element_type=jnp.float32)
    return (2.0 * first - product).astype(jnp.bfloat16)


def reference(activations, router_grad, token_ids, norm_terms, old_factors, old_router_factor, old_norm_diag, old_embed_diag):
    identity = jnp.eye(D, dtype=jnp.float32)
    inverses = []
    for index in range(NFAC):
        features = activations[index]
        fresh = jnp.dot(features.T, features, preferred_element_type=jnp.float32) / TOKENS
        matrix = factor_decay * old_factors[index] + (1.0 - factor_decay) * fresh + damping * identity
        inverses.append(newton_schulz(matrix))
    lefts = [jnp.dot(activations[m], inverses[m].T, preferred_element_type=jnp.float32).astype(jnp.bfloat16) for m in (0, 4, 6)]
    rights = [jnp.dot(activations[m], inverses[m], preferred_element_type=jnp.float32).astype(jnp.bfloat16) for m in (1, 2, 3, 5, 7)]
    pairs = ((0, 0), (0, 1), (0, 2), (1, 3))
    precond_attn = jnp.stack([learning_rate * jnp.dot(lefts[p].T, rights[w], preferred_element_type=jnp.float32) for p, w in pairs])
    router_fresh = jnp.dot(router_grad, router_grad.T, preferred_element_type=jnp.float32) / TOKENS
    router_matrix = factor_decay * old_router_factor + (1.0 - factor_decay) * router_fresh + damping * jnp.eye(EXPERTS, dtype=jnp.float32)
    router_inverse = newton_schulz(router_matrix)
    router_right = jnp.dot(router_grad.T, router_inverse, preferred_element_type=jnp.float32).astype(jnp.bfloat16)
    precond_router = learning_rate * jnp.dot(router_right.T, lefts[2], preferred_element_type=jnp.float32)
    norm_values = norm_terms.astype(jnp.float32)
    norm_total = jnp.sum(norm_values, axis=1)
    norm_squares = jnp.sum(norm_values * norm_values, axis=1)
    precond_norms = learning_rate * norm_total / (factor_decay * old_norm_diag + (1.0 - factor_decay) * (norm_squares / TOKENS) + damping)
    vocab_ids = jnp.arange(VOCAB, dtype=jnp.int32)
    onehot = (vocab_ids[:, None] == token_ids[None, :]).astype(jnp.bfloat16)
    embed_sum = jnp.dot(onehot, rights[4], preferred_element_type=jnp.float32)
    counts = jnp.sum(onehot, axis=1, dtype=jnp.float32)
    divisor = factor_decay * old_embed_diag + (1.0 - factor_decay) * (counts / TOKENS) + damping
    precond_embed = learning_rate * embed_sum / divisor[:, None]
    return (precond_attn, precond_router, precond_norms, precond_embed)
```

```python
import jax
import jax.numpy as jnp
from jax import lax
from jax.experimental import pallas as pl
from jax.experimental.pallas import tpu as pltpu
from jax.sharding import PartitionSpec as P

D = 2304
TOKENS = 2048
FEAT = 72
TOK = 256
WIDE = 576
HALF = 288
EXPERTS = 8
RATE = 0.05
RUN = 144
NT = (((1,), (1,)), ((), ()))
BF = jnp.bfloat16
F32 = jnp.float32


def here():
    s = lax.axis_index("shard")
    t = lax.axis_index("tensor")
    c = lax.axis_index("section")
    x, zl, y, k = lax.rem(s, 4), lax.div(s, 4), lax.div(c, 2), lax.rem(c, 2)
    return x, y, 2 * t + zl, k, zl, t


def at(x, y, z, k):
    return (lax.rem(z, 2) * 4 + x, lax.div(z, 2), 2 * y + k)


def step(v, d, n):
    return lax.rem(v + d, n)


def copy_to(src, dst, send, recv, device):
    return pltpu.make_async_remote_copy(
        src_ref=src,
        dst_ref=dst,
        send_sem=send,
        recv_sem=recv,
        device_id=device,
        device_id_type=pl.DeviceIdType.MESH,
    )


def signal(sem, device):
    pl.semaphore_signal(sem, inc=1, device_id=device, device_id_type=pl.DeviceIdType.MESH)


def precondition_kernel(
    feats, old, router_grad, ids, norm_terms, old_router, old_norm,
    out, rights, all_ids, norms,
    small, small_all,
    AT, OB, PM, PS, PR, MB, UB, UF, TR,
    z_send, z_recv, o_send, o_recv, ox_send, ox_recv, od_send, od_recv,
    p_send, p_recv, px_send, px_recv, u_send, u_recv, t_send, t_recv, s_send, s_recv,
):
    x, y, z, k, zl, t = here()
    s = zl * 4 + x
    me = at(x, y, z, k)
    xp, xm, xo = step(x, 1, 4), step(x, 3, 4), step(x, 2, 4)
    yp, ym, yo = step(y, 1, 4), step(y, 3, 4), step(y, 2, 4)
    east, west = at(xp, y, z, k), at(xm, y, z, k)
    north, south = at(x, yp, z, k), at(x, ym, z, k)
    partner = at(x, y, z, 1 - k)
    old_to = at(t, y, s, k)
    old_from = (z, x, 2 * y + k)
    old_stays = jnp.logical_and(x == t, z == s)

    barrier = pltpu.get_barrier_semaphore()
    for d in range(8):
        zz = step(z, d, 8)
        if d:
            signal(barrier, at(x, y, zz, k))
        signal(barrier, at(x, y, zz, 1 - k))
    for device in (east, west, north, south, at(x, yo, z, k)):
        signal(barrier, device)
    for d in range(1, 8):
        signal(barrier, (step(s, d, 8), t, 2 * y + k))

    @pl.when(jnp.logical_not(old_stays))
    def _():
        signal(barrier, old_to)
        signal(barrier, old_from)

    @pl.when(old_stays)
    def _():
        signal(barrier, partner)
        signal(barrier, partner)

    pl.semaphore_wait(barrier, 15 + 5 + 7 + 2)

    waits = []

    def rows_of(tt, yy, kk):
        return pl.ds(pl.multiple_of(tt * WIDE + yy * RUN + kk * FEAT, 8), FEAT)

    for d in range(8):
        zz = step(z, d, 8)
        src = feats.at[zz]
        dst = AT.at[x, rows_of(t, y, k), :]
        rsem = z_recv.at[2 * t + k]
        if d:
            cp = copy_to(src, dst, z_send.at[d], rsem, at(x, y, zz, zl))
            cp.start()
            waits.append(cp)
        else:

            @pl.when(k == zl)
            def _():
                pltpu.make_async_copy(src, dst, rsem).start()

            @pl.when(k != zl)
            def _():
                copy_to(src, dst, z_send.at[0], rsem, partner).start()

    old_dst = OB.at[t, pl.ds(pl.multiple_of(k * HALF, 16), HALF), :]

    @pl.when(old_stays)
    def _():
        pltpu.make_async_copy(old, old_dst, o_recv.at[0]).start()

    @pl.when(jnp.logical_not(old_stays))
    def _():
        copy_to(old, old_dst, o_send.at[0], o_recv.at[0], old_to).start()

    small[0:8, :] = router_grad[...].astype(F32)
    small[8:16, :] = jnp.broadcast_to(ids[...].astype(F32), (8, TOK))
    for i in range(2):
        terms = norm_terms[i].astype(F32)
        small[16 + i : 17 + i, 0:FEAT] = jnp.sum(terms, axis=0, keepdims=True)
        small[18 + i : 19 + i, 0:FEAT] = jnp.sum(terms * terms, axis=0, keepdims=True)
    for d in range(1, 8):
        cp = copy_to(small, small_all.at[s], s_send.at[d - 1], s_recv.at[s], (step(s, d, 8), t, 2 * y + k))
        cp.start()
        waits.append(cp)
    own_small = pltpu.make_async_copy(small, small_all.at[s], s_recv.at[s])
    own_small.start()

    def chunk(xx, yy, tt):
        return AT.at[xx, pl.ds(pl.multiple_of(tt * WIDE + yy * RUN, 16), RUN), :]

    n_sent = [0]

    def pass_on(xx, yy, tt, device):
        ref = chunk(xx, yy, tt)
        cp = copy_to(ref, ref, p_send.at[n_sent[0]], p_recv.at[xx * 16 + yy * 4 + tt], device)
        n_sent[0] += 1
        cp.start()
        waits.append(cp)

    def arrive(xx, yy, tt):
        ref = chunk(xx, yy, tt)
        copy_to(ref, ref, p_send.at[0], p_recv.at[xx * 16 + yy * 4 + tt], partner).wait_recv()

    for tt in range(4):
        for kk in range(2):
            ref = AT.at[x, rows_of(tt, y, kk), :]
            copy_to(ref, ref, z_send.at[0], z_recv.at[2 * tt + kk], partner).wait_recv()
        for device in (north, south, east, west) if tt < 2 else (east, west, north, south):
            pass_on(x, y, tt, device)

    def old_part(tt, kk, hh):
        start = kk * HALF + hh * RUN
        return OB.at[tt, pl.ds(pl.multiple_of(start, 16), RUN), :]

    def old_block(tt, kk):
        return OB.at[tt, pl.ds(pl.multiple_of(kk * HALF, 16), HALF), :]

    m_sent = [0]

    def old_on(tt, hh, device):
        ref = old_part(tt, k, hh)
        cp = copy_to(ref, ref, ox_send.at[m_sent[0]], ox_recv.at[2 * tt + hh], device)
        m_sent[0] += 1
        cp.start()
        waits.append(cp)

    def old_arrive(tt, hh):
        ref = old_part(tt, k, hh)
        copy_to(ref, ref, ox_send.at[0], ox_recv.at[2 * tt + hh], partner).wait_recv()

    def old_over(i, tt):
        ref = old_block(tt, k)
        cp = copy_to(ref, ref, od_send.at[i], od_recv.at[tt], partner)
        cp.start()
        waits.append(cp)

    pltpu.make_async_copy(old_block(x, k), old_block(x, k), o_recv.at[0]).wait()
    for hh in range(2):
        old_on(x, hh, east)
        old_on(x, hh, west)
    old_over(0, x)

    for tt in range(2):
        arrive(x, ym, tt)
        if tt == 0:
            pass_on(x, ym, tt, north)
        pass_on(x, ym, tt, east)
        pass_on(x, ym, tt, west)
        arrive(xm, y, 2 + tt)
        if tt == 0:
            pass_on(xm, y, 2, east)
        pass_on(xm, y, 2 + tt, north)
        pass_on(xm, y, 2 + tt, south)
    for tt in (1, 0):
        arrive(x, yp, tt)
        if tt == 1:
            pass_on(x, yp, tt, south)
        pass_on(x, yp, tt, east)
        pass_on(x, yp, tt, west)
        arrive(xp, y, 2 + tt)
        if tt == 1:
            pass_on(xp, y, 3, west)
        pass_on(xp, y, 2 + tt, north)
        pass_on(xp, y, 2 + tt, south)
    arrive(xm, y, 0)
    pass_on(xm, y, 0, east)
    arrive(xp, y, 1)
    pass_on(xp, y, 1, west)
    arrive(x, ym, 2)
    pass_on(x, ym, 2, north)
    arrive(x, yp, 3)
    pass_on(x, yp, 3, south)
    for tt in range(2):
        arrive(x, yo, tt)
        pass_on(x, yo, tt, east)
        pass_on(x, yo, tt, west)
        arrive(xo, y, 2 + tt)
        pass_on(xo, y, 2 + tt, north)
        pass_on(xo, y, 2 + tt, south)
    for hh in range(2):
        old_arrive(xm, hh)
        if hh == 0:
            old_on(xm, 0, east)
    old_over(1, xm)
    for hh in (1, 0):
        old_arrive(xp, hh)
        if hh == 1:
            old_on(xp, 1, west)
    old_over(2, xp)
    for aa in (1, 3, 2):
        yy, xx = step(y, aa, 4), step(x, aa, 4)
        arrive(xm, yy, 0)
        pass_on(xm, yy, 0, east)
        arrive(xp, yy, 1)
        pass_on(xp, yy, 1, west)
        arrive(xx, ym, 2)
        pass_on(xx, ym, 2, north)
        arrive(xx, yp, 3)
        pass_on(xx, yp, 3, south)
    for aa in range(4):
        yy, xx = step(y, aa, 4), step(x, aa, 4)
        arrive(xm, yy, 1)
        arrive(xp, yy, 0)
        arrive(xx, ym, 3)
        arrive(xx, yp, 2)
        arrive(xo, yy, 0)
        arrive(xo, yy, 1)
        arrive(xx, yo, 2)
        arrive(xx, yo, 3)
    for hh in range(2):
        old_arrive(xo, hh)
    old_over(3, xo)

    my_rows = pl.ds(pl.multiple_of(y * WIDE, 16), WIDE)

    @pl.loop(0, 4)
    def _(tt):
        block = pl.ds(pl.multiple_of(tt * WIDE, 16), WIDE)
        total = jnp.zeros((WIDE, WIDE), F32)
        for xx in range(4):
            total += lax.dot_general(AT[xx, my_rows, :], AT[xx, block, :], NT, preferred_element_type=F32)
        PM[tt] = total
        PS[tt] = total.astype(BF)
        copy_to(PS.at[tt], PR.at[tt], px_send.at[tt], px_recv.at[tt], partner).start()

    for aa in range(4):
        ref = old_block(step(x, aa, 4), 1 - k)
        copy_to(ref, ref, od_send.at[0], od_recv.at[step(x, aa, 4)], partner).wait_recv()

    TR[y] = jnp.zeros((8, 128), F32)
    row = lax.broadcasted_iota(jnp.int32, (WIDE, WIDE), 0) + y * WIDE
    col = lax.broadcasted_iota(jnp.int32, (WIDE, WIDE), 1)

    @pl.loop(0, 4)
    def _(tt):
        copy_to(PS.at[tt], PR.at[tt], px_send.at[tt], px_recv.at[tt], partner).wait()
        fresh = PM[tt] + PR[tt].astype(F32)
        eye = (row == col + tt * WIDE).astype(F32)
        matrix = 0.5 * OB[tt].astype(F32) + (0.5 / TOKENS) * fresh + 0.01 * eye
        TR[y] += jnp.full((8, 128), jnp.sum(matrix * eye), F32)
        MB[tt] = matrix.astype(BF)

    for i, dd in enumerate((1, 3, 2)):
        cp = copy_to(TR.at[y], TR.at[y], t_send.at[i], t_recv.at[y], at(x, step(y, dd, 4), z, k))
        cp.start()
        waits.append(cp)

    def times_matrix(block_of):
        total = jnp.zeros((WIDE, TOK), F32)
        for tt in range(4):
            total += jnp.dot(MB[tt], block_of(tt), preferred_element_type=F32)
        return total

    def spread(r):
        def part(yy, hh):
            return UB.at[r, yy, pl.ds(hh * HALF, HALF), :]

        def put(i, yy, hh, device):
            ref = part(yy, hh)
            cp = copy_to(ref, ref, u_send.at[6 * r + i], u_recv.at[8 * r + 2 * yy + hh], device)
            cp.start()
            waits.append(cp)

        def got(yy, hh):
            ref = part(yy, hh)
            copy_to(ref, ref, u_send.at[0], u_recv.at[8 * r + 2 * yy + hh], partner).wait_recv()

        put(0, y, 0, north)
        put(1, y, 1, south)
        put(2, y, 1, north)
        put(3, y, 0, south)
        got(ym, 0)
        put(4, ym, 0, north)
        got(yp, 1)
        put(5, yp, 1, south)
        got(ym, 1)
        got(yp, 0)
        got(yo, 0)
        got(yo, 1)

    u = times_matrix(lambda tt: AT[x, pl.ds(tt * WIDE, WIDE), :])
    UF[0] = u
    UB[0, y] = u.astype(BF)
    spread(0)
    u = times_matrix(lambda tt: UB[0, tt])
    UF[1] = u
    UB[1, y] = u.astype(BF)
    spread(1)
    u = times_matrix(lambda tt: UB[1, tt])
    for dd in range(1, 4):
        yy = step(y, dd, 4)
        copy_to(TR.at[yy], TR.at[yy], t_send.at[0], t_recv.at[yy], partner).wait_recv()
    trace = (TR[0] + TR[1] + TR[2] + TR[3])[0:1, 0:1]
    scale = D / (3.0 * trace)
    first = AT[x, my_rows, :].astype(F32)
    out[...] = (
        scale * (4.0 * first - scale * (6.0 * UF[0] - scale * (4.0 * UF[1] - scale * u)))
    ).astype(BF)

    for cp in waits:
        cp.wait_send()

    @pl.when(k != zl)
    def _():
        copy_to(feats.at[z], feats.at[z], z_send.at[0], z_recv.at[0], partner).wait_send()

    @pl.when(jnp.logical_not(old_stays))
    def _():
        copy_to(old, old_block(0, 0), o_send.at[0], o_recv.at[0], partner).wait_send()

    for d in range(8):
        ss = step(s, d, 8)
        copy_to(small, small_all.at[ss], s_send.at[0], s_recv.at[ss], partner).wait_recv()

    sums = jnp.zeros((EXPERTS, EXPERTS), F32)
    stats = jnp.zeros((8, TOK), F32)
    for ss in range(8):
        grad = small_all[ss, 0:8, :].astype(BF)
        sums += lax.dot_general(grad, grad, NT, preferred_element_type=F32)
        stats += small_all[ss, 16:24, :]
        all_ids[ss : ss + 1, :] = small_all[ss, 8:9, :]
    norms[...] = RATE * stats[0:2, 0:FEAT] / (
        0.5 * old_norm[...] + (0.5 / TOKENS) * stats[2:4, 0:FEAT] + 0.01
    )
    eye8 = (
        lax.broadcasted_iota(jnp.int32, (8, 8), 0) == lax.broadcasted_iota(jnp.int32, (8, 8), 1)
    ).astype(F32)
    matrix8 = 0.5 * old_router[...] + (0.5 / TOKENS) * sums + 0.01 * eye8
    scale8 = EXPERTS / (3.0 * jnp.sum(jnp.sum(matrix8 * eye8, axis=1, keepdims=True), axis=0, keepdims=True))
    low8 = matrix8.astype(BF)
    first8 = 2.0 * scale8 * eye8 - scale8 * scale8 * low8.astype(F32)
    image8 = jnp.dot(low8, first8.astype(BF), preferred_element_type=F32).astype(BF)
    inverse8 = (
        2.0 * first8 - jnp.dot(first8.astype(BF), image8, preferred_element_type=F32)
    ).astype(BF)
    mine = small_all[k * 4 + x, 0:8, :].astype(BF)
    rights[...] = lax.dot_general(
        inverse8, mine, (((0,), (0,)), ((), ())), preferred_element_type=F32
    ).astype(BF)


DMA = pltpu.SemaphoreType.DMA
VM = pl.BlockSpec(memory_space=pltpu.VMEM)


def precondition(*operands):
    return pl.pallas_call(
        precondition_kernel,
        out_shape=(
            jax.ShapeDtypeStruct((WIDE, TOK), BF),
            jax.ShapeDtypeStruct((8, TOK), BF),
            jax.ShapeDtypeStruct((8, TOK), F32),
            jax.ShapeDtypeStruct((2, FEAT), F32),
        ),
        in_specs=[VM] * 7,
        out_specs=[VM] * 4,
        scratch_shapes=[
            pltpu.VMEM((24, TOK), F32),
            pltpu.VMEM((8, 24, TOK), F32),
            pltpu.VMEM((4, D, TOK), BF),
            pltpu.VMEM((4, WIDE, WIDE), BF),
            pltpu.VMEM((4, WIDE, WIDE), F32),
            pltpu.VMEM((4, WIDE, WIDE), BF),
            pltpu.VMEM((4, WIDE, WIDE), BF),
            pltpu.VMEM((4, WIDE, WIDE), BF),
            pltpu.VMEM((2, 4, WIDE, TOK), BF),
            pltpu.VMEM((2, WIDE, TOK), F32),
            pltpu.VMEM((4, 8, 128), F32),
        ]
        + [DMA((n,)) for n in (8, 8, 1, 1, 6, 8, 4, 4, 60, 64, 4, 4, 12, 16, 3, 4, 7, 8)],
        compiler_params=pltpu.CompilerParams(
            collective_id=0, has_side_effects=True, vmem_limit_bytes=60 * 1024 * 1024
        ),
    )(*operands)


def combine_kernel(
    lt, rights,
    AO, EB, router,
    LB, RB, RX, PB, QB, SB, RSF, RSB, RP,
    l_send, l_recv, r_send, r_recv, b_send, c_send, c_recv, d_send, d_recv, q_send, q_recv,
    g_send, g_recv, e_send, e_recv, v_send, v_recv, n_send, n_recv, w_send, w_recv,
):
    x, y, z, k, zl, t = here()
    me = at(x, y, z, k)
    xp, xm, xo = step(x, 1, 4), step(x, 3, 4), step(x, 2, 4)
    yp, ym = step(y, 1, 4), step(y, 3, 4)
    east, west = at(xp, y, z, k), at(xm, y, z, k)
    north, south = at(x, yp, z, k), at(x, ym, z, k)
    partner = at(x, y, z, 1 - k)
    pair = at(x, y, 2 * t + 1 - zl, k)

    barrier = pltpu.get_barrier_semaphore()
    for dy in range(4):
        for dz in range(8):
            if dy or dz:
                signal(barrier, at(x, step(y, dy, 4), step(z, dz, 8), k))
    for dx in range(4):
        for kk in range(2):
            if dx or kk:
                signal(barrier, at(step(x, dx, 4), y, z, lax.rem(k + kk, 2)))
    pl.semaphore_wait(barrier, 31 + 7)

    pending = []

    def send(make, cond=None):
        if cond is None:
            make().start()
        else:

            @pl.when(cond)
            def _():
                make().start()

        pending.append((cond, make))

    def local(src, dst, sem, cond):
        @pl.when(cond)
        def _():
            pltpu.make_async_copy(src, dst, sem).start()

    def half(ref, hh, rows=HALF):
        return ref.at[pl.ds(hh * rows, rows), :]

    for i, (p, zz) in enumerate(((0, 0), (0, 1), (1, 1))):
        for hh in range(2):
            src, dst, rsem = half(lt, hh), half(LB.at[p], hh), l_recv.at[2 * p + hh]
            target = at(x, y, 2 * y + zz, k)
            cond = z == 4 * p
            if (p, zz) == (0, 0):
                local(src, dst, rsem, jnp.logical_and(cond, y == 0))
                cond = jnp.logical_and(cond, y != 0)
            send(
                lambda src=src, dst=dst, i=i, hh=hh, rsem=rsem, target=target: copy_to(
                    src, dst, l_send.at[2 * i + hh], rsem, target
                ),
                cond,
            )
    for w, zw in enumerate((1, 2, 3, 5)):
        for tt in range(4):
            zz = 2 * tt + w // 2
            dst, rsem = RB.at[w % 2], r_recv.at[w % 2]
            if zz == zw:
                local(lt, dst, rsem, z == zw)
            else:
                send(
                    lambda dst=dst, tt=tt, rsem=rsem, zz=zz: copy_to(
                        lt, dst, r_send.at[tt], rsem, at(x, y, zz, k)
                    ),
                    z == zw,
                )

    def piece(j):
        return RX.at[pl.ds(j * RUN, RUN), :]

    for j in range(4):
        src = half(lt, j, RUN)
        local(src, piece(j), c_recv.at[j], z == 7)
        for i, zz in enumerate((0, 6)):
            send(
                lambda src=src, j=j, i=i, zz=zz: copy_to(
                    src, piece(j), c_send.at[2 * j + i], c_recv.at[j], at(x, y, zz, k)
                ),
                z == 7,
            )
    is_router = z == 6

    @pl.when(is_router)
    def _():
        RP[k * 4 + x] = lax.dot_general(rights[...], lt[...], NT, preferred_element_type=F32)

    for i in range(1, 8):
        dx, kk = i // 2, i % 2
        send(
            lambda i=i, dx=dx, kk=kk: copy_to(
                RP.at[k * 4 + x], RP.at[k * 4 + x], n_send.at[i - 1], n_recv.at[k * 4 + x],
                at(step(x, dx, 4), y, z, lax.rem(k + kk, 2)),
            ),
            is_router,
        )

    def left_arrive(p, hh):
        pltpu.make_async_copy(half(LB.at[p], hh), half(LB.at[p], hh), l_recv.at[2 * p + hh]).wait()

    role = step(y - t, 4, 4)
    for p in range(2):

        def both(cond, p=p):
            return cond if p == 0 else jnp.logical_and(cond, zl == 1)

        def arrivals(p=p):
            left_arrive(p, 0)
            left_arrive(p, 1)

        if p == 0:
            arrivals()
        else:
            pl.when(zl == 1)(arrivals)

        def on(i, hh, device, p=p):
            ref = half(LB.at[p], hh)
            return copy_to(ref, ref, b_send.at[4 * p + i], l_recv.at[2 * p + hh], device)

        for i, (hh, device) in enumerate(((0, north), (1, south), (1, north), (0, south))):
            send(lambda i=i, hh=hh, device=device, on=on: on(i, hh, device), both(role == 0))
        send(lambda on=on: on(0, 0, north), both(role == 1))
        send(lambda on=on: on(0, 1, south), both(role == 3))

    for j in range(2):
        pltpu.make_async_copy(RB.at[j], RB.at[j], r_recv.at[j]).wait()
        left = LB[zl * j]
        theirs = RB[j, pl.ds(pl.multiple_of((1 - k) * HALF, 16), HALF), :]
        PB[j] = lax.dot_general(left, theirs, NT, preferred_element_type=F32).astype(BF)
        send(lambda j=j: copy_to(PB.at[j], QB.at[j], d_send.at[j], d_recv.at[j], partner))
        ours = RB[j, pl.ds(pl.multiple_of(k * HALF, 16), HALF), :]
        SB[j] = lax.dot_general(left, ours, NT, preferred_element_type=F32)

    def quarter(ref, xx):
        return ref.at[pl.ds(pl.multiple_of(xx * RUN, 16), RUN), :]

    for j in range(2):
        copy_to(PB.at[j], QB.at[j], d_send.at[j], d_recv.at[j], partner).wait_recv()
        total = SB[j] + QB[j].astype(F32)
        SB[j] = total
        RSF[j] = total.astype(BF)
        for i, dx in enumerate((1, 3, 2)):
            xx = step(x, dx, 4)
            send(
                lambda j=j, i=i, xx=xx: copy_to(
                    quarter(RSF.at[j], xx), RSB.at[j, x], q_send.at[3 * j + i], q_recv.at[4 * j + x],
                    at(xx, y, z, k),
                )
            )

    goes_on = jnp.logical_or(z <= 2, jnp.logical_or(z == 5, z == 6))
    z_next = jnp.where(z <= 2, z + 1, z - 1)
    z_next = jnp.where(goes_on, z_next, step(z, 1, 8))
    for j in range(4):
        pltpu.make_async_copy(piece(j), piece(j), c_recv.at[j]).wait()
        send(
            lambda j=j: copy_to(piece(j), piece(j), c_send.at[j], c_recv.at[j], at(x, y, z_next, k)),
            goes_on,
        )

    def result(w, xx):
        return AO.at[w, pl.ds(pl.multiple_of(xx * RUN, 16), RUN), :]

    for j in range(2):
        total = SB[j, pl.ds(pl.multiple_of(x * RUN, 16), RUN), :]
        for dx in range(1, 4):
            xx = step(x, dx, 4)
            copy_to(RSB.at[j, xx], RSB.at[j, xx], q_send.at[0], q_recv.at[4 * j + xx], partner).wait_recv()
            total += RSB[j, xx].astype(F32)
        w = 2 * zl + j
        AO[w, pl.ds(pl.multiple_of(x * RUN, 16), RUN), :] = (RATE * total).astype(BF)
        for i, device in enumerate((pair, east, west, at(xo, y, z, k))):
            send(
                lambda w=w, i=i, j=j, device=device: copy_to(
                    result(w, x), result(w, x), g_send.at[4 * j + i], g_recv.at[4 * w + x], device
                )
            )

    def result_arrive(w, xx):
        copy_to(result(w, xx), result(w, xx), g_send.at[0], g_recv.at[4 * w + xx], partner).wait_recv()

    for j in range(2):
        w = 2 * (1 - zl) + j
        result_arrive(w, x)
        for i, device in enumerate((east, west, at(xo, y, z, k))):
            send(
                lambda w=w, i=i, j=j, device=device: copy_to(
                    result(w, x), result(w, x), g_send.at[8 + 3 * j + i], g_recv.at[4 * w + x], device
                )
            )

    own = RX.at[pl.ds(pl.multiple_of(k * HALF, 16), HALF), :]
    other = RX.at[pl.ds(pl.multiple_of((1 - k) * HALF, 16), HALF), :]
    pltpu.make_async_copy(own, EB.at[x, k], v_recv.at[0]).start()
    send(lambda: copy_to(other, EB.at[x, k], v_send.at[0], v_recv.at[1], partner))
    pltpu.make_async_copy(own, EB.at[x, k], v_recv.at[0]).wait()

    def embed_part(xx, kk, hh):
        return EB.at[xx, kk, pl.ds(hh * RUN, RUN), :]

    n_e = [0]

    def embed_on(xx, kk, hh, device):
        i = n_e[0]
        n_e[0] += 1
        ref = embed_part(xx, kk, hh)
        send(lambda: copy_to(ref, ref, e_send.at[i], e_recv.at[xx * 4 + kk * 2 + hh], device))

    def embed_arrive(xx, kk, hh):
        ref = embed_part(xx, kk, hh)
        copy_to(ref, ref, e_send.at[0], e_recv.at[xx * 4 + kk * 2 + hh], partner).wait_recv()

    for kk in (k, 1 - k):
        if kk is not k:
            copy_to(own, EB.at[x, kk], v_send.at[0], v_recv.at[1], partner).wait_recv()
        for hh, device in ((0, east), (1, west), (1, east), (0, west)):
            embed_on(x, kk, hh, device)
    for kk in (k, 1 - k):
        embed_arrive(xm, kk, 0)
        embed_on(xm, kk, 0, east)
        embed_arrive(xp, kk, 1)
        embed_on(xp, kk, 1, west)

    @pl.when(is_router)
    def _():
        for i in range(1, 8):
            ss = step(k * 4 + x, i, 8)
            copy_to(RP.at[ss], RP.at[ss], n_send.at[0], n_recv.at[ss], partner).wait_recv()
        total = jnp.zeros((8, WIDE), F32)
        for ss in range(8):
            total += RP[ss]
        RP[8] = RATE * total

    for dy in range(4):
        for zz in range(2):
            yy, z_to = step(y, dy, 4), 2 * y + zz
            cond = is_router
            if dy == 0 and zz == 0:
                stays = jnp.logical_and(is_router, y == 3)
                local(RP.at[8], router, w_recv.at[0], stays)
                cond = jnp.logical_and(is_router, y != 3)
            send(
                lambda dy=dy, zz=zz, yy=yy, z_to=z_to: copy_to(
                    RP.at[8], router, w_send.at[2 * dy + zz], w_recv.at[0], at(x, yy, z_to, k)
                ),
                cond,
            )

    for kk in (k, 1 - k):
        for xx, hh in ((xm, 1), (xp, 0), (xo, 0), (xo, 1)):
            embed_arrive(xx, kk, hh)
    for dx in (1, 3, 2):
        for w in range(4):
            result_arrive(w, step(x, dx, 4))
    pltpu.make_async_copy(router, router, w_recv.at[0]).wait()
    for cond, make in pending:
        if cond is None:
            make().wait_send()
        else:

            @pl.when(cond)
            def _(make=make):
                make().wait_send()


def combine(lt, rights):
    return pl.pallas_call(
        combine_kernel,
        out_shape=(
            jax.ShapeDtypeStruct((4, WIDE, HALF), BF),
            jax.ShapeDtypeStruct((4, 2, HALF, TOK), BF),
            jax.ShapeDtypeStruct((8, WIDE), F32),
        ),
        in_specs=[VM] * 2,
        out_specs=[VM] * 3,
        scratch_shapes=[
            pltpu.VMEM((2, WIDE, TOK), BF),
            pltpu.VMEM((2, WIDE, TOK), BF),
            pltpu.VMEM((WIDE, TOK), BF),
            pltpu.VMEM((2, WIDE, HALF), BF),
            pltpu.VMEM((2, WIDE, HALF), BF),
            pltpu.VMEM((2, WIDE, HALF), F32),
            pltpu.VMEM((2, WIDE, HALF), BF),
            pltpu.VMEM((2, 4, RUN, HALF), BF),
            pltpu.VMEM((9, 8, WIDE), F32),
        ]
        + [DMA((n,)) for n in (6, 4, 4, 2, 8, 8, 4, 2, 2, 6, 8, 14, 16, 12, 16, 1, 2, 7, 8, 8, 1)],
        compiler_params=pltpu.CompilerParams(
            collective_id=1, has_side_effects=True, vmem_limit_bytes=60 * 1024 * 1024
        ),
    )(lt, rights)


STEP = 512


def finish_kernel(AO, EB, router_in, ids, norms_in, diag, attn, embed, router, norms):
    i = pl.program_id(0)
    t = lax.axis_index("tensor")
    attn[...] = AO[...].astype(F32)
    router[...] = router_in[...]
    norms[...] = norms_in[...]
    start = (t * (8192 // 4) + i * STEP).astype(F32)
    vocab = lax.broadcasted_iota(jnp.int32, (STEP, TOK), 0).astype(F32) + start
    total = jnp.zeros((STEP, HALF), F32)
    counts = jnp.zeros((STEP, TOK), F32)
    for xx in range(4):
        for kk in range(2):
            hit = (vocab == ids[kk * 4 + xx : kk * 4 + xx + 1, :]).astype(F32)
            counts += hit
            total += lax.dot_general(hit.astype(BF), EB[xx, kk], NT, preferred_element_type=F32)
    count = jnp.sum(counts, axis=1, keepdims=True)
    divisor = 0.5 * diag[...] + (0.5 / TOKENS) * count + 0.01
    embed[...] = RATE * total / divisor


def finish(AO, EB, router, ids, norms, diag):
    whole = lambda a: pl.BlockSpec(a.shape, lambda i: (0,) * a.ndim)
    return pl.pallas_call(
        finish_kernel,
        grid=(4,),
        out_shape=(
            jax.ShapeDtypeStruct((4, WIDE, HALF), F32),
            jax.ShapeDtypeStruct((2048, HALF), F32),
            jax.ShapeDtypeStruct((8, WIDE), F32),
            jax.ShapeDtypeStruct((2, FEAT), F32),
        ),
        in_specs=[
            pl.BlockSpec((1, WIDE, HALF), lambda i: (i, 0, 0)),
            whole(EB),
            whole(router),
            whole(ids),
            whole(norms),
            pl.BlockSpec((STEP, 1), lambda i: (i, 0)),
        ],
        out_specs=[
            pl.BlockSpec((1, WIDE, HALF), lambda i: (i, 0, 0)),
            pl.BlockSpec((STEP, HALF), lambda i: (i, 0)),
            pl.BlockSpec((8, WIDE), lambda i: (0, 0)),
            pl.BlockSpec((2, FEAT), lambda i: (0, 0)),
        ],
    )(AO, EB, router, ids, norms, diag)


def per_device(
    activations,
    router_grad,
    token_ids,
    norm_terms,
    old_factors,
    old_router_factor,
    old_norm_diag,
    old_embed_diag,
):
    feats = jnp.transpose(activations, (0, 2, 1))
    old = jnp.transpose(old_factors[0].astype(BF))
    lt, rights, ids, norms = precondition(
        feats, old, router_grad, token_ids[None, :], norm_terms, old_router_factor, old_norm_diag
    )
    AO, EB, router = combine(lt, rights)
    attn, embed, router, norms = finish(AO, EB, router, ids, norms, old_embed_diag[:, None])
    return attn, router, norms, embed


def solution(mesh):
    return jax.shard_map(
        per_device,
        mesh=mesh,
        in_specs=(
            P(None, "shard", ("tensor", "section")),
            P(None, "shard"),
            P("shard"),
            P(None, "shard", ("tensor", "section")),
            P("shard", "tensor", "section"),
            P(),
            P(None, ("tensor", "section")),
            P("tensor"),
        ),
        out_specs=(
            P(None, "tensor", "section"),
            P(None, "tensor"),
            P(None, ("tensor", "section")),
            P("tensor", "section"),
        ),
        check_vma=False,
    )
```

```python
import jax
import jax.numpy as jnp
from jax import lax
from jax.experimental import pallas as pl
from jax.experimental.pallas import tpu as pltpu
from jax.sharding import PartitionSpec as P

D = 2304
TOKENS = 2048
FEAT = 72
TOK = 256
WIDE = 576
HALF = 288
EXPERTS = 8
RATE = 0.05
RUN = 144
NT = (((1,), (1,)), ((), ()))
BF = jnp.bfloat16
F32 = jnp.float32


def here():
    s = lax.axis_index("shard")
    t = lax.axis_index("tensor")
    c = lax.axis_index("section")
    x, zl, y, k = lax.rem(s, 4), lax.div(s, 4), lax.div(c, 2), lax.rem(c, 2)
    return x, y, 2 * t + zl, k, zl, t


def at(x, y, z, k):
    return (lax.rem(z, 2) * 4 + x, lax.div(z, 2), 2 * y + k)


def step(v, d, n):
    return lax.rem(v + d, n)


def copy_to(src, dst, send, recv, device):
    return pltpu.make_async_remote_copy(
        src_ref=src,
        dst_ref=dst,
        send_sem=send,
        recv_sem=recv,
        device_id=device,
        device_id_type=pl.DeviceIdType.MESH,
    )


def signal(sem, device):
    pl.semaphore_signal(sem, inc=1, device_id=device, device_id_type=pl.DeviceIdType.MESH)


def precondition_kernel(
    feats, old, router_grad, ids, norm_terms, old_router, old_norm,
    out, rights, all_ids, norms,
    small, small_all,
    AT, OB, PM, PS, PR, MB, UB, UF, TR,
    z_send, z_recv, o_send, o_recv, ox_send, ox_recv, od_send, od_recv,
    p_send, p_recv, px_send, px_recv, u_send, u_recv, t_send, t_recv, s_send, s_recv,
):
    x, y, z, k, zl, t = here()
    s = zl * 4 + x
    me = at(x, y, z, k)
    xp, xm, xo = step(x, 1, 4), step(x, 3, 4), step(x, 2, 4)
    yp, ym, yo = step(y, 1, 4), step(y, 3, 4), step(y, 2, 4)
    east, west = at(xp, y, z, k), at(xm, y, z, k)
    north, south = at(x, yp, z, k), at(x, ym, z, k)
    partner = at(x, y, z, 1 - k)
    old_to = at(t, y, s, k)
    old_from = (z, x, 2 * y + k)
    old_stays = jnp.logical_and(x == t, z == s)

    barrier = pltpu.get_barrier_semaphore()
    for d in range(8):
        zz = step(z, d, 8)
        if d:
            signal(barrier, at(x, y, zz, k))
        signal(barrier, at(x, y, zz, 1 - k))
    for device in (east, west, north, south, at(x, yo, z, k)):
        signal(barrier, device)
    for d in range(1, 8):
        signal(barrier, (step(s, d, 8), t, 2 * y + k))

    @pl.when(jnp.logical_not(old_stays))
    def _():
        signal(barrier, old_to)
        signal(barrier, old_from)

    @pl.when(old_stays)
    def _():
        signal(barrier, partner)
        signal(barrier, partner)

    pl.semaphore_wait(barrier, 15 + 5 + 7 + 2)

    waits = []

    def rows_of(tt, yy, kk):
        return pl.ds(pl.multiple_of(tt * WIDE + yy * RUN + kk * FEAT, 8), FEAT)

    for d in range(8):
        zz = step(z, d, 8)
        src = feats.at[zz]
        dst = AT.at[x, rows_of(t, y, k), :]
        rsem = z_recv.at[2 * t + k]
        if d:
            cp = copy_to(src, dst, z_send.at[d], rsem, at(x, y, zz, zl))
            cp.start()
            waits.append(cp)
        else:

            @pl.when(k == zl)
            def _():
                pltpu.make_async_copy(src, dst, rsem).start()

            @pl.when(k != zl)
            def _():
                copy_to(src, dst, z_send.at[0], rsem, partner).start()

    old_dst = OB.at[t, pl.ds(pl.multiple_of(k * HALF, 16), HALF), :]

    @pl.when(old_stays)
    def _():
        pltpu.make_async_copy(old, old_dst, o_recv.at[0]).start()

    @pl.when(jnp.logical_not(old_stays))
    def _():
        copy_to(old, old_dst, o_send.at[0], o_recv.at[0], old_to).start()

    small[0:8, :] = router_grad[...].astype(F32)
    small[8:16, :] = jnp.broadcast_to(ids[...].astype(F32), (8, TOK))
    for i in range(2):
        terms = norm_terms[i].astype(F32)
        small[16 + i : 17 + i, 0:FEAT] = jnp.sum(terms, axis=0, keepdims=True)
        small[18 + i : 19 + i, 0:FEAT] = jnp.sum(terms * terms, axis=0, keepdims=True)
    for d in range(1, 8):
        cp = copy_to(small, small_all.at[s], s_send.at[d - 1], s_recv.at[s], (step(s, d, 8), t, 2 * y + k))
        cp.start()
        waits.append(cp)
    own_small = pltpu.make_async_copy(small, small_all.at[s], s_recv.at[s])
    own_small.start()

    def chunk(xx, yy, tt):
        return AT.at[xx, pl.ds(pl.multiple_of(tt * WIDE + yy * RUN, 16), RUN), :]

    n_sent = [0]

    def pass_on(xx, yy, tt, device):
        ref = chunk(xx, yy, tt)
        cp = copy_to(ref, ref, p_send.at[n_sent[0]], p_recv.at[xx * 16 + yy * 4 + tt], device)
        n_sent[0] += 1
        cp.start()
        waits.append(cp)

    def arrive(xx, yy, tt):
        ref = chunk(xx, yy, tt)
        copy_to(ref, ref, p_send.at[0], p_recv.at[xx * 16 + yy * 4 + tt], partner).wait_recv()

    for tt in range(4):
        for kk in range(2):
            ref = AT.at[x, rows_of(tt, y, kk), :]
            copy_to(ref, ref, z_send.at[0], z_recv.at[2 * tt + kk], partner).wait_recv()
        for device in (north, south, east, west) if tt < 2 else (east, west, north, south):
            pass_on(x, y, tt, device)

    def old_part(tt, kk, hh):
        start = kk * HALF + hh * RUN
        return OB.at[tt, pl.ds(pl.multiple_of(start, 16), RUN), :]

    def old_block(tt, kk):
        return OB.at[tt, pl.ds(pl.multiple_of(kk * HALF, 16), HALF), :]

    m_sent = [0]

    def old_on(tt, hh, device):
        ref = old_part(tt, k, hh)
        cp = copy_to(ref, ref, ox_send.at[m_sent[0]], ox_recv.at[2 * tt + hh], device)
        m_sent[0] += 1
        cp.start()
        waits.append(cp)

    def old_arrive(tt, hh):
        ref = old_part(tt, k, hh)
        copy_to(ref, ref, ox_send.at[0], ox_recv.at[2 * tt + hh], partner).wait_recv()

    def old_over(i, tt):
        ref = old_block(tt, k)
        cp = copy_to(ref, ref, od_send.at[i], od_recv.at[tt], partner)
        cp.start()
        waits.append(cp)

    pltpu.make_async_copy(old_block(x, k), old_block(x, k), o_recv.at[0]).wait()
    for hh in range(2):
        old_on(x, hh, east)
        old_on(x, hh, west)
    old_over(0, x)

    for tt in range(2):
        arrive(x, ym, tt)
        if tt == 0:
            pass_on(x, ym, tt, north)
        pass_on(x, ym, tt, east)
        pass_on(x, ym, tt, west)
        arrive(xm, y, 2 + tt)
        if tt == 0:
            pass_on(xm, y, 2, east)
        pass_on(xm, y, 2 + tt, north)
        pass_on(xm, y, 2 + tt, south)
    for tt in (1, 0):
        arrive(x, yp, tt)
        if tt == 1:
            pass_on(x, yp, tt, south)
        pass_on(x, yp, tt, east)
        pass_on(x, yp, tt, west)
        arrive(xp, y, 2 + tt)
        if tt == 1:
            pass_on(xp, y, 3, west)
        pass_on(xp, y, 2 + tt, north)
        pass_on(xp, y, 2 + tt, south)
    arrive(xm, y, 0)
    pass_on(xm, y, 0, east)
    arrive(xp, y, 1)
    pass_on(xp, y, 1, west)
    arrive(x, ym, 2)
    pass_on(x, ym, 2, north)
    arrive(x, yp, 3)
    pass_on(x, yp, 3, south)
    for tt in range(2):
        arrive(x, yo, tt)
        pass_on(x, yo, tt, east)
        pass_on(x, yo, tt, west)
        arrive(xo, y, 2 + tt)
        pass_on(xo, y, 2 + tt, north)
        pass_on(xo, y, 2 + tt, south)
    for hh in range(2):
        old_arrive(xm, hh)
        if hh == 0:
            old_on(xm, 0, east)
    old_over(1, xm)
    for hh in (1, 0):
        old_arrive(xp, hh)
        if hh == 1:
            old_on(xp, 1, west)
    old_over(2, xp)
    for aa in (1, 3, 2):
        yy, xx = step(y, aa, 4), step(x, aa, 4)
        arrive(xm, yy, 0)
        pass_on(xm, yy, 0, east)
        arrive(xp, yy, 1)
        pass_on(xp, yy, 1, west)
        arrive(xx, ym, 2)
        pass_on(xx, ym, 2, north)
        arrive(xx, yp, 3)
        pass_on(xx, yp, 3, south)
    for aa in range(4):
        yy, xx = step(y, aa, 4), step(x, aa, 4)
        arrive(xm, yy, 1)
        arrive(xp, yy, 0)
        arrive(xx, ym, 3)
        arrive(xx, yp, 2)
        arrive(xo, yy, 0)
        arrive(xo, yy, 1)
        arrive(xx, yo, 2)
        arrive(xx, yo, 3)
    for hh in range(2):
        old_arrive(xo, hh)
    old_over(3, xo)

    my_rows = pl.ds(pl.multiple_of(y * WIDE, 16), WIDE)

    @pl.loop(0, 4)
    def _(tt):
        block = pl.ds(pl.multiple_of(tt * WIDE, 16), WIDE)
        total = jnp.zeros((WIDE, WIDE), F32)
        for xx in range(4):
            total += lax.dot_general(AT[xx, my_rows, :], AT[xx, block, :], NT, preferred_element_type=F32)
        PM[tt] = total
        PS[tt] = total.astype(BF)
        copy_to(PS.at[tt], PR.at[tt], px_send.at[tt], px_recv.at[tt], partner).start()

    for aa in range(4):
        ref = old_block(step(x, aa, 4), 1 - k)
        copy_to(ref, ref, od_send.at[0], od_recv.at[step(x, aa, 4)], partner).wait_recv()

    TR[y] = jnp.zeros((8, 128), F32)
    row = lax.broadcasted_iota(jnp.int32, (WIDE, WIDE), 0) + y * WIDE
    col = lax.broadcasted_iota(jnp.int32, (WIDE, WIDE), 1)

    @pl.loop(0, 4)
    def _(tt):
        copy_to(PS.at[tt], PR.at[tt], px_send.at[tt], px_recv.at[tt], partner).wait()
        fresh = PM[tt] + PR[tt].astype(F32)
        eye = (row == col + tt * WIDE).astype(F32)
        matrix = 0.5 * OB[tt].astype(F32) + (0.5 / TOKENS) * fresh + 0.01 * eye
        TR[y] += jnp.full((8, 128), jnp.sum(matrix * eye), F32)
        MB[tt] = matrix.astype(BF)

    for i, dd in enumerate((1, 3, 2)):
        cp = copy_to(TR.at[y], TR.at[y], t_send.at[i], t_recv.at[y], at(x, step(y, dd, 4), z, k))
        cp.start()
        waits.append(cp)

    def times_matrix(block_of):
        total = jnp.zeros((WIDE, TOK), F32)
        for tt in range(4):
            total += jnp.dot(MB[tt], block_of(tt), preferred_element_type=F32)
        return total

    def spread(r):
        def part(yy, hh):
            return UB.at[r, yy, pl.ds(hh * HALF, HALF), :]

        def put(i, yy, hh, device):
            ref = part(yy, hh)
            cp = copy_to(ref, ref, u_send.at[6 * r + i], u_recv.at[8 * r + 2 * yy + hh], device)
            cp.start()
            waits.append(cp)

        def got(yy, hh):
            ref = part(yy, hh)
            copy_to(ref, ref, u_send.at[0], u_recv.at[8 * r + 2 * yy + hh], partner).wait_recv()

        put(0, y, 0, north)
        put(1, y, 1, south)
        put(2, y, 1, north)
        put(3, y, 0, south)
        got(ym, 0)
        put(4, ym, 0, north)
        got(yp, 1)
        put(5, yp, 1, south)
        got(ym, 1)
        got(yp, 0)
        got(yo, 0)
        got(yo, 1)

    u = times_matrix(lambda tt: AT[x, pl.ds(tt * WIDE, WIDE), :])
    UF[0] = u
    UB[0, y] = u.astype(BF)
    spread(0)
    u = times_matrix(lambda tt: UB[0, tt])
    UF[1] = u
    UB[1, y] = u.astype(BF)
    spread(1)
    u = times_matrix(lambda tt: UB[1, tt])
    for dd in range(1, 4):
        yy = step(y, dd, 4)
        copy_to(TR.at[yy], TR.at[yy], t_send.at[0], t_recv.at[yy], partner).wait_recv()
    trace = (TR[0] + TR[1] + TR[2] + TR[3])[0:1, 0:1]
    scale = D / (3.0 * trace)
    first = AT[x, my_rows, :].astype(F32)
    out[...] = (
        scale * (4.0 * first - scale * (6.0 * UF[0] - scale * (4.0 * UF[1] - scale * u)))
    ).astype(BF)

    for cp in waits:
        cp.wait_send()

    @pl.when(k != zl)
    def _():
        copy_to(feats.at[z], feats.at[z], z_send.at[0], z_recv.at[0], partner).wait_send()

    @pl.when(jnp.logical_not(old_stays))
    def _():
        copy_to(old, old_block(0, 0), o_send.at[0], o_recv.at[0], partner).wait_send()

    for d in range(8):
        ss = step(s, d, 8)
        copy_to(small, small_all.at[ss], s_send.at[0], s_recv.at[ss], partner).wait_recv()

    sums = jnp.zeros((EXPERTS, EXPERTS), F32)
    stats = jnp.zeros((8, TOK), F32)
    for ss in range(8):
        grad = small_all[ss, 0:8, :].astype(BF)
        sums += lax.dot_general(grad, grad, NT, preferred_element_type=F32)
        stats += small_all[ss, 16:24, :]
        all_ids[ss : ss + 1, :] = small_all[ss, 8:9, :]
    norms[...] = RATE * stats[0:2, 0:FEAT] / (
        0.5 * old_norm[...] + (0.5 / TOKENS) * stats[2:4, 0:FEAT] + 0.01
    )
    eye8 = (
        lax.broadcasted_iota(jnp.int32, (8, 8), 0) == lax.broadcasted_iota(jnp.int32, (8, 8), 1)
    ).astype(F32)
    matrix8 = 0.5 * old_router[...] + (0.5 / TOKENS) * sums + 0.01 * eye8
    scale8 = EXPERTS / (3.0 * jnp.sum(jnp.sum(matrix8 * eye8, axis=1, keepdims=True), axis=0, keepdims=True))
    low8 = matrix8.astype(BF)
    first8 = 2.0 * scale8 * eye8 - scale8 * scale8 * low8.astype(F32)
    image8 = jnp.dot(low8, first8.astype(BF), preferred_element_type=F32).astype(BF)
    inverse8 = (
        2.0 * first8 - jnp.dot(first8.astype(BF), image8, preferred_element_type=F32)
    ).astype(BF)
    mine = small_all[k * 4 + x, 0:8, :].astype(BF)
    rights[...] = lax.dot_general(
        inverse8, mine, (((0,), (0,)), ((), ())), preferred_element_type=F32
    ).astype(BF)


DMA = pltpu.SemaphoreType.DMA
VM = pl.BlockSpec(memory_space=pltpu.VMEM)


def precondition(*operands):
    return pl.pallas_call(
        precondition_kernel,
        out_shape=(
            jax.ShapeDtypeStruct((WIDE, TOK), BF),
            jax.ShapeDtypeStruct((8, TOK), BF),
            jax.ShapeDtypeStruct((8, TOK), F32),
            jax.ShapeDtypeStruct((2, FEAT), F32),
        ),
        in_specs=[VM] * 7,
        out_specs=[VM] * 4,
        scratch_shapes=[
            pltpu.VMEM((24, TOK), F32),
            pltpu.VMEM((8, 24, TOK), F32),
            pltpu.VMEM((4, D, TOK), BF),
            pltpu.VMEM((4, WIDE, WIDE), BF),
            pltpu.VMEM((4, WIDE, WIDE), F32),
            pltpu.VMEM((4, WIDE, WIDE), BF),
            pltpu.VMEM((4, WIDE, WIDE), BF),
            pltpu.VMEM((4, WIDE, WIDE), BF),
            pltpu.VMEM((2, 4, WIDE, TOK), BF),
            pltpu.VMEM((2, WIDE, TOK), F32),
            pltpu.VMEM((4, 8, 128), F32),
        ]
        + [DMA((n,)) for n in (8, 8, 1, 1, 6, 8, 4, 4, 60, 64, 4, 4, 12, 16, 3, 4, 7, 8)],
        compiler_params=pltpu.CompilerParams(
            collective_id=0, has_side_effects=True, vmem_limit_bytes=60 * 1024 * 1024
        ),
    )(*operands)


def combine_kernel(
    lt, rights,
    AO, EB, router,
    LB, RB, RX, PB, QB, SB, RSF, RSB, RP,
    l_send, l_recv, r_send, r_recv, b_send, c_send, c_recv, d_send, d_recv, q_send, q_recv,
    g_send, g_recv, e_send, e_recv, v_send, v_recv, n_send, n_recv, w_send, w_recv,
):
    x, y, z, k, zl, t = here()
    me = at(x, y, z, k)
    xp, xm, xo = step(x, 1, 4), step(x, 3, 4), step(x, 2, 4)
    yp, ym = step(y, 1, 4), step(y, 3, 4)
    east, west = at(xp, y, z, k), at(xm, y, z, k)
    north, south = at(x, yp, z, k), at(x, ym, z, k)
    partner = at(x, y, z, 1 - k)
    pair = at(x, y, 2 * t + 1 - zl, k)

    barrier = pltpu.get_barrier_semaphore()
    for dy in range(4):
        for dz in range(8):
            if dy or dz:
                signal(barrier, at(x, step(y, dy, 4), step(z, dz, 8), k))
    for dx in range(4):
        for kk in range(2):
            if dx or kk:
                signal(barrier, at(step(x, dx, 4), y, z, lax.rem(k + kk, 2)))
    pl.semaphore_wait(barrier, 31 + 7)

    pending = []

    def send(make, cond=None):
        if cond is None:
            make().start()
        else:

            @pl.when(cond)
            def _():
                make().start()

        pending.append((cond, make))

    def local(src, dst, sem, cond):
        @pl.when(cond)
        def _():
            pltpu.make_async_copy(src, dst, sem).start()

    def half(ref, hh, rows=HALF):
        return ref.at[pl.ds(hh * rows, rows), :]

    for i, (p, zz) in enumerate(((0, 0), (0, 1), (1, 1))):
        for hh in range(2):
            src, dst, rsem = half(lt, hh), half(LB.at[p], hh), l_recv.at[2 * p + hh]
            target = at(x, y, 2 * y + zz, k)
            cond = z == 4 * p
            if (p, zz) == (0, 0):
                local(src, dst, rsem, jnp.logical_and(cond, y == 0))
                cond = jnp.logical_and(cond, y != 0)
            send(
                lambda src=src, dst=dst, i=i, hh=hh, rsem=rsem, target=target: copy_to(
                    src, dst, l_send.at[2 * i + hh], rsem, target
                ),
                cond,
            )
    for w, zw in enumerate((1, 2, 3, 5)):
        for tt in range(4):
            zz = 2 * tt + w // 2
            dst, rsem = RB.at[w % 2], r_recv.at[w % 2]
            if zz == zw:
                local(lt, dst, rsem, z == zw)
            else:
                send(
                    lambda dst=dst, tt=tt, rsem=rsem, zz=zz: copy_to(
                        lt, dst, r_send.at[tt], rsem, at(x, y, zz, k)
                    ),
                    z == zw,
                )

    def piece(j):
        return RX.at[pl.ds(j * RUN, RUN), :]

    for j in range(4):
        src = half(lt, j, RUN)
        local(src, piece(j), c_recv.at[j], z == 7)
        for i, zz in enumerate((0, 6)):
            send(
                lambda src=src, j=j, i=i, zz=zz: copy_to(
                    src, piece(j), c_send.at[2 * j + i], c_recv.at[j], at(x, y, zz, k)
                ),
                z == 7,
            )
    is_router = z == 6

    @pl.when(is_router)
    def _():
        RP[k * 4 + x] = lax.dot_general(rights[...], lt[...], NT, preferred_element_type=F32)

    for i in range(1, 8):
        dx, kk = i // 2, i % 2
        send(
            lambda i=i, dx=dx, kk=kk: copy_to(
                RP.at[k * 4 + x], RP.at[k * 4 + x], n_send.at[i - 1], n_recv.at[k * 4 + x],
                at(step(x, dx, 4), y, z, lax.rem(k + kk, 2)),
            ),
            is_router,
        )

    goes_on = jnp.logical_or(z <= 2, jnp.logical_or(z == 5, z == 6))
    z_next = jnp.where(z <= 2, z + 1, z - 1)
    z_next = jnp.where(goes_on, z_next, step(z, 1, 8))
    for j in range(4):
        pltpu.make_async_copy(piece(j), piece(j), c_recv.at[j]).wait()
        send(
            lambda j=j: copy_to(piece(j), piece(j), c_send.at[j], c_recv.at[j], at(x, y, z_next, k)),
            goes_on,
        )

    def left_arrive(p, hh):
        pltpu.make_async_copy(half(LB.at[p], hh), half(LB.at[p], hh), l_recv.at[2 * p + hh]).wait()

    role = step(y - t, 4, 4)
    for p in range(2):

        def both(cond, p=p):
            return cond if p == 0 else jnp.logical_and(cond, zl == 1)

        def arrivals(p=p):
            left_arrive(p, 0)
            left_arrive(p, 1)

        if p == 0:
            arrivals()
        else:
            pl.when(zl == 1)(arrivals)

        def on(i, hh, device, p=p):
            ref = half(LB.at[p], hh)
            return copy_to(ref, ref, b_send.at[4 * p + i], l_recv.at[2 * p + hh], device)

        for i, (hh, device) in enumerate(((0, north), (1, south), (1, north), (0, south))):
            send(lambda i=i, hh=hh, device=device, on=on: on(i, hh, device), both(role == 0))
        send(lambda on=on: on(0, 0, north), both(role == 1))
        send(lambda on=on: on(0, 1, south), both(role == 3))

    own = RX.at[pl.ds(pl.multiple_of(k * HALF, 16), HALF), :]
    other = RX.at[pl.ds(pl.multiple_of((1 - k) * HALF, 16), HALF), :]
    pltpu.make_async_copy(own, EB.at[x, k], v_recv.at[0]).start()
    send(lambda: copy_to(other, EB.at[x, k], v_send.at[0], v_recv.at[1], partner))
    pltpu.make_async_copy(own, EB.at[x, k], v_recv.at[0]).wait()

    def embed_part(xx, kk, hh):
        return EB.at[xx, kk, pl.ds(hh * RUN, RUN), :]

    n_e = [0]

    def embed_on(xx, kk, hh, device):
        i = n_e[0]
        n_e[0] += 1
        ref = embed_part(xx, kk, hh)
        send(lambda: copy_to(ref, ref, e_send.at[i], e_recv.at[xx * 4 + kk * 2 + hh], device))

    def embed_arrive(xx, kk, hh):
        ref = embed_part(xx, kk, hh)
        copy_to(ref, ref, e_send.at[0], e_recv.at[xx * 4 + kk * 2 + hh], partner).wait_recv()

    for kk in (k, 1 - k):
        if kk is not k:
            copy_to(own, EB.at[x, kk], v_send.at[0], v_recv.at[1], partner).wait_recv()
        for hh, device in ((0, east), (1, west), (1, east), (0, west)):
            embed_on(x, kk, hh, device)
    for j in range(2):
        pltpu.make_async_copy(RB.at[j], RB.at[j], r_recv.at[j]).wait()
        left = LB[zl * j]
        theirs = RB[j, pl.ds(pl.multiple_of((1 - k) * HALF, 16), HALF), :]
        PB[j] = lax.dot_general(theirs, left, NT, preferred_element_type=F32).astype(BF)
        send(lambda j=j: copy_to(PB.at[j], QB.at[j], d_send.at[j], d_recv.at[j], partner))
        ours = RB[j, pl.ds(pl.multiple_of(k * HALF, 16), HALF), :]
        SB[j] = lax.dot_general(ours, left, NT, preferred_element_type=F32)

    def quarter(ref, xx):
        return ref.at[pl.ds(pl.multiple_of(xx * FEAT, 8), FEAT), :]

    for j in range(2):
        copy_to(PB.at[j], QB.at[j], d_send.at[j], d_recv.at[j], partner).wait_recv()
        total = SB[j] + QB[j].astype(F32)
        SB[j] = total
        RSF[j] = total.astype(BF)
        for i, dx in enumerate((1, 3, 2)):
            xx = step(x, dx, 4)
            send(
                lambda j=j, i=i, xx=xx: copy_to(
                    quarter(RSF.at[j], xx), RSB.at[j, x], q_send.at[3 * j + i], q_recv.at[4 * j + x],
                    at(xx, y, z, k),
                )
            )

    for kk in (k, 1 - k):
        embed_arrive(xm, kk, 0)
        embed_on(xm, kk, 0, east)
        embed_arrive(xp, kk, 1)
        embed_on(xp, kk, 1, west)

    def result(w, xx):
        return AO.at[w, pl.ds(pl.multiple_of(xx * FEAT, 8), FEAT), :]

    for j in range(2):
        total = SB[j, pl.ds(pl.multiple_of(x * FEAT, 8), FEAT), :]
        for dx in range(1, 4):
            xx = step(x, dx, 4)
            copy_to(RSB.at[j, xx], RSB.at[j, xx], q_send.at[0], q_recv.at[4 * j + xx], partner).wait_recv()
            total += RSB[j, xx].astype(F32)
        w = 2 * zl + j
        AO[w, pl.ds(pl.multiple_of(x * FEAT, 8), FEAT), :] = (RATE * total).astype(BF)
        for i, device in enumerate((pair, east, west)):
            send(
                lambda w=w, i=i, j=j, device=device: copy_to(
                    result(w, x), result(w, x), g_send.at[3 * j + i], g_recv.at[4 * w + x], device
                )
            )

    def result_arrive(w, xx):
        copy_to(result(w, xx), result(w, xx), g_send.at[0], g_recv.at[4 * w + xx], partner).wait_recv()

    for j in range(2):
        w = 2 * (1 - zl) + j
        result_arrive(w, x)
        for i, device in enumerate((east, west)):
            send(
                lambda w=w, i=i, j=j, device=device: copy_to(
                    result(w, x), result(w, x), g_send.at[6 + 2 * j + i], g_recv.at[4 * w + x], device
                )
            )

    def result_part(w, xx, hh):
        return AO.at[w, pl.ds(pl.multiple_of(xx * FEAT + hh * 40, 8), (40, 32)[hh]), :]

    for i, w in enumerate((2 * zl, 2 * zl + 1, 2 * (1 - zl), 2 * (1 - zl) + 1)):
        for hh, xx, device in ((0, xm, east), (1, xp, west)):
            result_arrive(w, xx)
            send(
                lambda w=w, i=i, hh=hh, xx=xx, device=device: copy_to(
                    result_part(w, xx, hh), result_part(w, xx, hh), g_send.at[10 + 2 * i + hh],
                    g_recv.at[16 + 2 * w + hh], device,
                )
            )

    @pl.when(is_router)
    def _():
        for i in range(1, 8):
            ss = step(k * 4 + x, i, 8)
            copy_to(RP.at[ss], RP.at[ss], n_send.at[0], n_recv.at[ss], partner).wait_recv()
        total = jnp.zeros((8, WIDE), F32)
        for ss in range(8):
            total += RP[ss]
        RP[8] = RATE * total

    for dy in range(4):
        for zz in range(2):
            yy, z_to = step(y, dy, 4), 2 * y + zz
            cond = is_router
            if dy == 0 and zz == 0:
                stays = jnp.logical_and(is_router, y == 3)
                local(RP.at[8], router, w_recv.at[0], stays)
                cond = jnp.logical_and(is_router, y != 3)
            send(
                lambda dy=dy, zz=zz, yy=yy, z_to=z_to: copy_to(
                    RP.at[8], router, w_send.at[2 * dy + zz], w_recv.at[0], at(x, yy, z_to, k)
                ),
                cond,
            )

    for kk in (k, 1 - k):
        for xx, hh in ((xm, 1), (xp, 0), (xo, 0), (xo, 1)):
            embed_arrive(xx, kk, hh)
    for w in range(4):
        for hh in range(2):
            ref = result_part(w, xo, hh)
            copy_to(ref, ref, g_send.at[0], g_recv.at[16 + 2 * w + hh], partner).wait_recv()
    pltpu.make_async_copy(router, router, w_recv.at[0]).wait()
    for cond, make in pending:
        if cond is None:
            make().wait_send()
        else:

            @pl.when(cond)
            def _(make=make):
                make().wait_send()


def combine(lt, rights):
    return pl.pallas_call(
        combine_kernel,
        out_shape=(
            jax.ShapeDtypeStruct((4, HALF, WIDE), BF),
            jax.ShapeDtypeStruct((4, 2, HALF, TOK), BF),
            jax.ShapeDtypeStruct((8, WIDE), F32),
        ),
        in_specs=[VM] * 2,
        out_specs=[VM] * 3,
        scratch_shapes=[
            pltpu.VMEM((2, WIDE, TOK), BF),
            pltpu.VMEM((2, WIDE, TOK), BF),
            pltpu.VMEM((WIDE, TOK), BF),
            pltpu.VMEM((2, HALF, WIDE), BF),
            pltpu.VMEM((2, HALF, WIDE), BF),
            pltpu.VMEM((2, HALF, WIDE), F32),
            pltpu.VMEM((2, HALF, WIDE), BF),
            pltpu.VMEM((2, 4, FEAT, WIDE), BF),
            pltpu.VMEM((9, 8, WIDE), F32),
        ]
        + [DMA((n,)) for n in (6, 4, 4, 2, 8, 8, 4, 2, 2, 6, 8, 18, 24, 12, 16, 1, 2, 7, 8, 8, 1)],
        compiler_params=pltpu.CompilerParams(
            collective_id=1, has_side_effects=True, vmem_limit_bytes=60 * 1024 * 1024
        ),
    )(lt, rights)


STEP = 512


def finish_kernel(AO, EB, router_in, ids, norms_in, diag, attn, embed, router, norms):
    i = pl.program_id(0)
    t = lax.axis_index("tensor")
    attn[...] = AO[...].astype(F32)
    router[...] = router_in[...]
    norms[...] = norms_in[...]
    start = (t * (8192 // 4) + i * STEP).astype(F32)
    vocab = lax.broadcasted_iota(jnp.int32, (STEP, TOK), 0).astype(F32) + start
    total = jnp.zeros((HALF, STEP), F32)
    counts = jnp.zeros((STEP, TOK), F32)
    for xx in range(4):
        for kk in range(2):
            hit = (vocab == ids[kk * 4 + xx : kk * 4 + xx + 1, :]).astype(F32)
            counts += hit
            total += lax.dot_general(EB[xx, kk], hit.astype(BF), NT, preferred_element_type=F32)
    ones = jnp.ones((8, TOK), BF)
    count = lax.dot_general(ones, counts.astype(BF), NT, preferred_element_type=F32)[0:1, :]
    divisor = 0.5 * diag[...] + (0.5 / TOKENS) * count + 0.01
    embed[...] = total * (RATE / divisor)


def finish(AO, EB, router, ids, norms, diag):
    whole = lambda a: pl.BlockSpec(a.shape, lambda i: (0,) * a.ndim)
    return pl.pallas_call(
        finish_kernel,
        grid=(4,),
        out_shape=(
            jax.ShapeDtypeStruct((4, HALF, WIDE), F32),
            jax.ShapeDtypeStruct((HALF, 2048), F32),
            jax.ShapeDtypeStruct((8, WIDE), F32),
            jax.ShapeDtypeStruct((2, FEAT), F32),
        ),
        in_specs=[
            pl.BlockSpec((1, HALF, WIDE), lambda i: (i, 0, 0)),
            whole(EB),
            whole(router),
            whole(ids),
            whole(norms),
            pl.BlockSpec((1, STEP), lambda i: (0, i)),
        ],
        out_specs=[
            pl.BlockSpec((1, HALF, WIDE), lambda i: (i, 0, 0)),
            pl.BlockSpec((HALF, STEP), lambda i: (0, i)),
            pl.BlockSpec((8, WIDE), lambda i: (0, 0)),
            pl.BlockSpec((2, FEAT), lambda i: (0, 0)),
        ],
    )(AO, EB, router, ids, norms, diag)


def per_device(
    activations,
    router_grad,
    token_ids,
    norm_terms,
    old_factors,
    old_router_factor,
    old_norm_diag,
    old_embed_diag,
):
    feats = jnp.transpose(activations, (0, 2, 1))
    old = jnp.transpose(old_factors[0].astype(BF))
    lt, rights, ids, norms = precondition(
        feats, old, router_grad, token_ids[None, :], norm_terms, old_router_factor, old_norm_diag
    )
    AO, EB, router = combine(lt, rights)
    attn, embed, router, norms = finish(AO, EB, router, ids, norms, old_embed_diag[None, :])
    return jnp.transpose(attn, (0, 2, 1)), router, norms, jnp.transpose(embed)


def solution(mesh):
    return jax.shard_map(
        per_device,
        mesh=mesh,
        in_specs=(
            P(None, "shard", ("tensor", "section")),
            P(None, "shard"),
            P("shard"),
            P(None, "shard", ("tensor", "section")),
            P("shard", "tensor", "section"),
            P(),
            P(None, ("tensor", "section")),
            P("tensor"),
        ),
        out_specs=(
            P(None, "tensor", "section"),
            P(None, "tensor"),
            P(None, ("tensor", "section")),
            P("tensor", "section"),
        ),
        check_vma=False,
    )
```

```python
import jax
import jax.numpy as jnp
from jax import lax
from jax.experimental import pallas as pl
from jax.experimental.pallas import tpu as pltpu
from jax.sharding import PartitionSpec as P

D = 2304
TOKENS = 2048
FEAT = 72
TOK = 256
WIDE = 576
HALF = 288
EXPERTS = 8
RATE = 0.05
RUN = 144
NT = (((1,), (1,)), ((), ()))
BF = jnp.bfloat16
F32 = jnp.float32


def here():
    s = lax.axis_index("shard")
    t = lax.axis_index("tensor")
    c = lax.axis_index("section")
    x, zl, y, k = lax.rem(s, 4), lax.div(s, 4), lax.div(c, 2), lax.rem(c, 2)
    return x, y, 2 * t + zl, k, zl, t


def at(x, y, z, k):
    return (lax.rem(z, 2) * 4 + x, lax.div(z, 2), 2 * y + k)


def step(v, d, n):
    return lax.rem(v + d, n)


def copy_to(src, dst, send, recv, device):
    return pltpu.make_async_remote_copy(
        src_ref=src,
        dst_ref=dst,
        send_sem=send,
        recv_sem=recv,
        device_id=device,
        device_id_type=pl.DeviceIdType.MESH,
    )


def signal(sem, device):
    pl.semaphore_signal(sem, inc=1, device_id=device, device_id_type=pl.DeviceIdType.MESH)


def precondition_kernel(
    feats, old, router_grad, ids, norm_terms, old_router, old_norm,
    out, rights, all_ids, norms,
    small, small_all,
    AT, OB, PM, PS, PR, MB, UB, UF, TR,
    z_send, z_recv, o_send, o_recv, ox_send, ox_recv, od_send, od_recv,
    p_send, p_recv, px_send, px_recv, u_send, u_recv, t_send, t_recv, s_send, s_recv,
):
    x, y, z, k, zl, t = here()
    s = zl * 4 + x
    me = at(x, y, z, k)
    xp, xm, xo = step(x, 1, 4), step(x, 3, 4), step(x, 2, 4)
    yp, ym, yo = step(y, 1, 4), step(y, 3, 4), step(y, 2, 4)
    east, west = at(xp, y, z, k), at(xm, y, z, k)
    north, south = at(x, yp, z, k), at(x, ym, z, k)
    partner = at(x, y, z, 1 - k)
    old_to = at(t, y, s, k)
    old_from = (z, x, 2 * y + k)
    old_stays = jnp.logical_and(x == t, z == s)

    barrier = pltpu.get_barrier_semaphore()
    for d in range(8):
        zz = step(z, d, 8)
        if d:
            signal(barrier, at(x, y, zz, k))
        signal(barrier, at(x, y, zz, 1 - k))
    for device in (east, west, north, south, at(x, yo, z, k)):
        signal(barrier, device)
    for d in range(1, 8):
        signal(barrier, (step(s, d, 8), t, 2 * y + k))

    @pl.when(jnp.logical_not(old_stays))
    def _():
        signal(barrier, old_to)
        signal(barrier, old_from)

    @pl.when(old_stays)
    def _():
        signal(barrier, partner)
        signal(barrier, partner)

    for dy in range(4):
        for dz in range(8):
            if dy or dz:
                signal(barrier, at(x, step(y, dy, 4), step(z, dz, 8), k))
    for dx in range(4):
        for kk in range(2):
            if dx or kk:
                signal(barrier, at(step(x, dx, 4), y, z, lax.rem(k + kk, 2)))
    pl.semaphore_wait(barrier, 15 + 5 + 7 + 2 + 31 + 7)

    waits = []

    def rows_of(tt, yy, kk):
        return pl.ds(pl.multiple_of(tt * WIDE + yy * RUN + kk * FEAT, 8), FEAT)

    for d in range(8):
        zz = step(z, d, 8)
        src = feats.at[zz]
        dst = AT.at[x, rows_of(t, y, k), :]
        rsem = z_recv.at[2 * t + k]
        if d:
            cp = copy_to(src, dst, z_send.at[d], rsem, at(x, y, zz, zl))
            cp.start()
            waits.append(cp)
        else:

            @pl.when(k == zl)
            def _():
                pltpu.make_async_copy(src, dst, rsem).start()

            @pl.when(k != zl)
            def _():
                copy_to(src, dst, z_send.at[0], rsem, partner).start()

    old_dst = OB.at[t, pl.ds(pl.multiple_of(k * HALF, 16), HALF), :]

    @pl.when(old_stays)
    def _():
        pltpu.make_async_copy(old, old_dst, o_recv.at[0]).start()

    @pl.when(jnp.logical_not(old_stays))
    def _():
        copy_to(old, old_dst, o_send.at[0], o_recv.at[0], old_to).start()

    small[0:8, :] = router_grad[...].astype(F32)
    small[8:16, :] = jnp.broadcast_to(ids[...].astype(F32), (8, TOK))
    for i in range(2):
        terms = norm_terms[i].astype(F32)
        small[16 + i : 17 + i, 0:FEAT] = jnp.sum(terms, axis=0, keepdims=True)
        small[18 + i : 19 + i, 0:FEAT] = jnp.sum(terms * terms, axis=0, keepdims=True)
    for d in range(1, 8):
        cp = copy_to(small, small_all.at[s], s_send.at[d - 1], s_recv.at[s], (step(s, d, 8), t, 2 * y + k))
        cp.start()
        waits.append(cp)
    own_small = pltpu.make_async_copy(small, small_all.at[s], s_recv.at[s])
    own_small.start()

    def chunk(xx, yy, tt):
        return AT.at[xx, pl.ds(pl.multiple_of(tt * WIDE + yy * RUN, 16), RUN), :]

    n_sent = [0]

    def pass_on(xx, yy, tt, device):
        ref = chunk(xx, yy, tt)
        cp = copy_to(ref, ref, p_send.at[n_sent[0]], p_recv.at[xx * 16 + yy * 4 + tt], device)
        n_sent[0] += 1
        cp.start()
        waits.append(cp)

    def arrive(xx, yy, tt):
        ref = chunk(xx, yy, tt)
        copy_to(ref, ref, p_send.at[0], p_recv.at[xx * 16 + yy * 4 + tt], partner).wait_recv()

    for tt in range(4):
        for kk in range(2):
            ref = AT.at[x, rows_of(tt, y, kk), :]
            copy_to(ref, ref, z_send.at[0], z_recv.at[2 * tt + kk], partner).wait_recv()
        for device in (north, south, east, west) if tt < 2 else (east, west, north, south):
            pass_on(x, y, tt, device)

    def old_part(tt, kk, hh):
        start = kk * HALF + hh * RUN
        return OB.at[tt, pl.ds(pl.multiple_of(start, 16), RUN), :]

    def old_block(tt, kk):
        return OB.at[tt, pl.ds(pl.multiple_of(kk * HALF, 16), HALF), :]

    m_sent = [0]

    def old_on(tt, hh, device):
        ref = old_part(tt, k, hh)
        cp = copy_to(ref, ref, ox_send.at[m_sent[0]], ox_recv.at[2 * tt + hh], device)
        m_sent[0] += 1
        cp.start()
        waits.append(cp)

    def old_arrive(tt, hh):
        ref = old_part(tt, k, hh)
        copy_to(ref, ref, ox_send.at[0], ox_recv.at[2 * tt + hh], partner).wait_recv()

    def old_over(i, tt):
        ref = old_block(tt, k)
        cp = copy_to(ref, ref, od_send.at[i], od_recv.at[tt], partner)
        cp.start()
        waits.append(cp)

    pltpu.make_async_copy(old_block(x, k), old_block(x, k), o_recv.at[0]).wait()
    for hh in range(2):
        old_on(x, hh, east)
        old_on(x, hh, west)
    old_over(0, x)

    for tt in range(2):
        arrive(x, ym, tt)
        if tt == 0:
            pass_on(x, ym, tt, north)
        pass_on(x, ym, tt, east)
        pass_on(x, ym, tt, west)
        arrive(xm, y, 2 + tt)
        if tt == 0:
            pass_on(xm, y, 2, east)
        pass_on(xm, y, 2 + tt, north)
        pass_on(xm, y, 2 + tt, south)
    for tt in (1, 0):
        arrive(x, yp, tt)
        if tt == 1:
            pass_on(x, yp, tt, south)
        pass_on(x, yp, tt, east)
        pass_on(x, yp, tt, west)
        arrive(xp, y, 2 + tt)
        if tt == 1:
            pass_on(xp, y, 3, west)
        pass_on(xp, y, 2 + tt, north)
        pass_on(xp, y, 2 + tt, south)
    arrive(xm, y, 0)
    pass_on(xm, y, 0, east)
    arrive(xp, y, 1)
    pass_on(xp, y, 1, west)
    arrive(x, ym, 2)
    pass_on(x, ym, 2, north)
    arrive(x, yp, 3)
    pass_on(x, yp, 3, south)
    for tt in range(2):
        arrive(x, yo, tt)
        pass_on(x, yo, tt, east)
        pass_on(x, yo, tt, west)
        arrive(xo, y, 2 + tt)
        pass_on(xo, y, 2 + tt, north)
        pass_on(xo, y, 2 + tt, south)
    for hh in range(2):
        old_arrive(xm, hh)
        if hh == 0:
            old_on(xm, 0, east)
    old_over(1, xm)
    for hh in (1, 0):
        old_arrive(xp, hh)
        if hh == 1:
            old_on(xp, 1, west)
    old_over(2, xp)
    for aa in (1, 3, 2):
        yy, xx = step(y, aa, 4), step(x, aa, 4)
        arrive(xm, yy, 0)
        pass_on(xm, yy, 0, east)
        arrive(xp, yy, 1)
        pass_on(xp, yy, 1, west)
        arrive(xx, ym, 2)
        pass_on(xx, ym, 2, north)
        arrive(xx, yp, 3)
        pass_on(xx, yp, 3, south)
    for aa in range(4):
        yy, xx = step(y, aa, 4), step(x, aa, 4)
        arrive(xm, yy, 1)
        arrive(xp, yy, 0)
        arrive(xx, ym, 3)
        arrive(xx, yp, 2)
        arrive(xo, yy, 0)
        arrive(xo, yy, 1)
        arrive(xx, yo, 2)
        arrive(xx, yo, 3)
    for hh in range(2):
        old_arrive(xo, hh)
    old_over(3, xo)

    my_rows = pl.ds(pl.multiple_of(y * WIDE, 16), WIDE)

    @pl.loop(0, 4)
    def _(tt):
        block = pl.ds(pl.multiple_of(tt * WIDE, 16), WIDE)
        total = jnp.zeros((WIDE, WIDE), F32)
        for xx in range(4):
            total += lax.dot_general(AT[xx, my_rows, :], AT[xx, block, :], NT, preferred_element_type=F32)
        PM[tt] = total
        PS[tt] = total.astype(BF)
        copy_to(PS.at[tt], PR.at[tt], px_send.at[tt], px_recv.at[tt], partner).start()

    for aa in range(4):
        ref = old_block(step(x, aa, 4), 1 - k)
        copy_to(ref, ref, od_send.at[0], od_recv.at[step(x, aa, 4)], partner).wait_recv()

    TR[y] = jnp.zeros((8, 128), F32)
    row = lax.broadcasted_iota(jnp.int32, (WIDE, WIDE), 0) + y * WIDE
    col = lax.broadcasted_iota(jnp.int32, (WIDE, WIDE), 1)

    @pl.loop(0, 4)
    def _(tt):
        copy_to(PS.at[tt], PR.at[tt], px_send.at[tt], px_recv.at[tt], partner).wait()
        fresh = PM[tt] + PR[tt].astype(F32)
        eye = (row == col + tt * WIDE).astype(F32)
        matrix = 0.5 * OB[tt].astype(F32) + (0.5 / TOKENS) * fresh + 0.01 * eye
        TR[y] += jnp.full((8, 128), jnp.sum(matrix * eye), F32)
        MB[tt] = matrix.astype(BF)

    for i, dd in enumerate((1, 3, 2)):
        cp = copy_to(TR.at[y], TR.at[y], t_send.at[i], t_recv.at[y], at(x, step(y, dd, 4), z, k))
        cp.start()
        waits.append(cp)

    def shared_values():
        for d in range(8):
            ss = step(s, d, 8)
            copy_to(small, small_all.at[ss], s_send.at[0], s_recv.at[ss], partner).wait_recv()

        sums = jnp.zeros((EXPERTS, EXPERTS), F32)
        stats = jnp.zeros((8, TOK), F32)
        for ss in range(8):
            grad = small_all[ss, 0:8, :].astype(BF)
            sums += lax.dot_general(grad, grad, NT, preferred_element_type=F32)
            stats += small_all[ss, 16:24, :]
            all_ids[ss : ss + 1, :] = small_all[ss, 8:9, :]
        norms[...] = RATE * stats[0:2, 0:FEAT] / (
            0.5 * old_norm[...] + (0.5 / TOKENS) * stats[2:4, 0:FEAT] + 0.01
        )
        eye8 = (
            lax.broadcasted_iota(jnp.int32, (8, 8), 0) == lax.broadcasted_iota(jnp.int32, (8, 8), 1)
        ).astype(F32)
        matrix8 = 0.5 * old_router[...] + (0.5 / TOKENS) * sums + 0.01 * eye8
        scale8 = EXPERTS / (3.0 * jnp.sum(jnp.sum(matrix8 * eye8, axis=1, keepdims=True), axis=0, keepdims=True))
        low8 = matrix8.astype(BF)
        first8 = 2.0 * scale8 * eye8 - scale8 * scale8 * low8.astype(F32)
        image8 = jnp.dot(low8, first8.astype(BF), preferred_element_type=F32).astype(BF)
        inverse8 = (
            2.0 * first8 - jnp.dot(first8.astype(BF), image8, preferred_element_type=F32)
        ).astype(BF)
        mine = small_all[k * 4 + x, 0:8, :].astype(BF)
        rights[...] = lax.dot_general(
            inverse8, mine, (((0,), (0,)), ((), ())), preferred_element_type=F32
        ).astype(BF)

    def spread_times(r):
        def part(yy, hh):
            return UB.at[r, yy, pl.ds(hh * HALF, HALF), :]

        def put(i, yy, hh, device):
            ref = part(yy, hh)
            cp = copy_to(ref, ref, u_send.at[6 * r + i], u_recv.at[8 * r + 2 * yy + hh], device)
            cp.start()
            waits.append(cp)

        def got(yy, hh):
            ref = part(yy, hh)
            copy_to(ref, ref, u_send.at[0], u_recv.at[8 * r + 2 * yy + hh], partner).wait_recv()

        def term(yy):
            return jnp.dot(MB[yy], UB[r, yy], preferred_element_type=F32)

        put(0, y, 0, north)
        put(1, y, 1, south)
        put(2, y, 1, north)
        put(3, y, 0, south)
        total = term(y)
        if r == 0:
            shared_values()
        got(ym, 0)
        put(4, ym, 0, north)
        got(yp, 1)
        put(5, yp, 1, south)
        got(ym, 1)
        total += term(ym)
        got(yp, 0)
        total += term(yp)
        got(yo, 0)
        got(yo, 1)
        return total + term(yo)

    u = jnp.zeros((WIDE, TOK), F32)
    for tt in range(4):
        u += jnp.dot(MB[tt], AT[x, pl.ds(tt * WIDE, WIDE), :], preferred_element_type=F32)
    UF[0] = u
    UB[0, y] = u.astype(BF)
    u = spread_times(0)
    UF[1] = u
    UB[1, y] = u.astype(BF)
    u = spread_times(1)
    for dd in range(1, 4):
        yy = step(y, dd, 4)
        copy_to(TR.at[yy], TR.at[yy], t_send.at[0], t_recv.at[yy], partner).wait_recv()
    trace = (TR[0] + TR[1] + TR[2] + TR[3])[0:1, 0:1]
    scale = D / (3.0 * trace)
    first = AT[x, my_rows, :].astype(F32)
    out[...] = (
        scale * (4.0 * first - scale * (6.0 * UF[0] - scale * (4.0 * UF[1] - scale * u)))
    ).astype(BF)

    def settle():
        for cp in waits:
            cp.wait_send()

        @pl.when(k != zl)
        def _():
            copy_to(feats.at[z], feats.at[z], z_send.at[0], z_recv.at[0], partner).wait_send()

        @pl.when(jnp.logical_not(old_stays))
        def _():
            copy_to(old, old_block(0, 0), o_send.at[0], o_recv.at[0], partner).wait_send()

    return settle


DMA = pltpu.SemaphoreType.DMA
VM = pl.BlockSpec(memory_space=pltpu.VMEM)


def combine_kernel(
    lt, rights,
    AO, EB, router,
    LB, RB, RX, PB, QB, SB, RSF, RSB, RP,
    l_send, l_recv, r_send, r_recv, b_send, c_send, c_recv, d_send, d_recv, q_send, q_recv,
    g_send, g_recv, e_send, e_recv, v_send, v_recv, n_send, n_recv, w_send, w_recv,
):
    x, y, z, k, zl, t = here()
    me = at(x, y, z, k)
    xp, xm, xo = step(x, 1, 4), step(x, 3, 4), step(x, 2, 4)
    yp, ym = step(y, 1, 4), step(y, 3, 4)
    east, west = at(xp, y, z, k), at(xm, y, z, k)
    north, south = at(x, yp, z, k), at(x, ym, z, k)
    partner = at(x, y, z, 1 - k)
    pair = at(x, y, 2 * t + 1 - zl, k)

    pending = []

    def send(make, cond=None):
        if cond is None:
            make().start()
        else:

            @pl.when(cond)
            def _():
                make().start()

        pending.append((cond, make))

    def local(src, dst, sem, cond):
        @pl.when(cond)
        def _():
            pltpu.make_async_copy(src, dst, sem).start()

    def half(ref, hh, rows=HALF):
        return ref.at[pl.ds(hh * rows, rows), :]

    for i, (p, zz) in enumerate(((0, 0), (0, 1), (1, 1))):
        for hh in range(2):
            src, dst, rsem = half(lt, hh), half(LB.at[p], hh), l_recv.at[2 * p + hh]
            target = at(x, y, 2 * y + zz, k)
            cond = z == 4 * p
            if (p, zz) == (0, 0):
                local(src, dst, rsem, jnp.logical_and(cond, y == 0))
                cond = jnp.logical_and(cond, y != 0)
            send(
                lambda src=src, dst=dst, i=i, hh=hh, rsem=rsem, target=target: copy_to(
                    src, dst, l_send.at[2 * i + hh], rsem, target
                ),
                cond,
            )
    for w, (zw, first) in enumerate(((1, (2, 0)), (2, (4, 0)), (3, (5, 1)), (5, (7, 3)))):
        j = w % 2
        for hh in range(2):
            src, dst, rsem = half(lt, hh), half(RB.at[j], hh), r_recv.at[2 * j + hh]
            if w:
                local(src, dst, rsem, z == zw)
            for i, zz in enumerate(first):
                send(
                    lambda src=src, dst=dst, rsem=rsem, i=i, hh=hh, zz=zz: copy_to(
                        src, dst, r_send.at[2 * hh + i], rsem, at(x, y, zz, k)
                    ),
                    z == zw,
                )

    def right_arrive(j, hh):
        ref = half(RB.at[j], hh)
        pltpu.make_async_copy(ref, ref, r_recv.at[2 * j + hh]).wait()

    def right_on(j, hh, cond, to):
        pl.when(cond)(lambda: right_arrive(j, hh))
        ref = half(RB.at[j], hh)
        send(
            lambda: copy_to(ref, ref, r_send.at[4 + 2 * j + hh], r_recv.at[2 * j + hh], at(x, y, to, k)),
            cond,
        )

    def among(*planes):
        found = z == planes[0]
        for p in planes[1:]:
            found = jnp.logical_or(found, z == p)
        return found


    def piece(j):
        return RX.at[pl.ds(j * RUN, RUN), :]

    for j in range(4):
        src = half(lt, j, RUN)
        local(src, piece(j), c_recv.at[j], z == 7)
        for i, zz in enumerate((0, 6)):
            send(
                lambda src=src, j=j, i=i, zz=zz: copy_to(
                    src, piece(j), c_send.at[2 * j + i], c_recv.at[j], at(x, y, zz, k)
                ),
                z == 7,
            )
    is_router = z == 6

    @pl.when(is_router)
    def _():
        RP[k * 4 + x] = lax.dot_general(rights[...], lt[...], NT, preferred_element_type=F32)

    for i in range(1, 8):
        dx, kk = i // 2, i % 2
        send(
            lambda i=i, dx=dx, kk=kk: copy_to(
                RP.at[k * 4 + x], RP.at[k * 4 + x], n_send.at[i - 1], n_recv.at[k * 4 + x],
                at(step(x, dx, 4), y, z, lax.rem(k + kk, 2)),
            ),
            is_router,
        )

    goes_on = jnp.logical_or(z <= 2, jnp.logical_or(z == 5, z == 6))
    z_next = jnp.where(z <= 2, z + 1, z - 1)
    z_next = jnp.where(goes_on, z_next, step(z, 1, 8))
    for j in range(4):
        pltpu.make_async_copy(piece(j), piece(j), c_recv.at[j]).wait()
        send(
            lambda j=j: copy_to(piece(j), piece(j), c_send.at[j], c_recv.at[j], at(x, y, z_next, k)),
            goes_on,
        )

    on00, on01, on10, on11 = among(0, 2, 5), among(0, 1, 6), among(3, 4), among(0, 7)
    right_on(0, 0, on00, jnp.where(z == 0, 6, jnp.where(z == 2, 4, 7)))
    right_on(1, 0, on10, jnp.where(z == 4, 6, 1))
    right_on(1, 1, on11, jnp.where(z == 0, 6, 1))
    right_on(0, 1, on01, jnp.where(z == 0, 6, jnp.where(z == 1, 7, 4)))

    def left_arrive(p, hh):
        pltpu.make_async_copy(half(LB.at[p], hh), half(LB.at[p], hh), l_recv.at[2 * p + hh]).wait()

    role = step(y - t, 4, 4)
    for p in range(2):

        def both(cond, p=p):
            return cond if p == 0 else jnp.logical_and(cond, zl == 1)

        def arrivals(p=p):
            left_arrive(p, 0)
            left_arrive(p, 1)

        if p == 0:
            arrivals()
        else:
            pl.when(zl == 1)(arrivals)

        def on(i, hh, device, p=p):
            ref = half(LB.at[p], hh)
            return copy_to(ref, ref, b_send.at[4 * p + i], l_recv.at[2 * p + hh], device)

        for i, (hh, device) in enumerate(((0, north), (1, south), (1, north), (0, south))):
            send(lambda i=i, hh=hh, device=device, on=on: on(i, hh, device), both(role == 0))
        send(lambda on=on: on(0, 0, north), both(role == 1))
        send(lambda on=on: on(0, 1, south), both(role == 3))

    own = RX.at[pl.ds(pl.multiple_of(k * HALF, 16), HALF), :]
    other = RX.at[pl.ds(pl.multiple_of((1 - k) * HALF, 16), HALF), :]
    pltpu.make_async_copy(own, EB.at[x, k], v_recv.at[0]).start()
    send(lambda: copy_to(other, EB.at[x, k], v_send.at[0], v_recv.at[1], partner))
    pltpu.make_async_copy(own, EB.at[x, k], v_recv.at[0]).wait()

    def embed_part(xx, kk, hh):
        return EB.at[xx, kk, pl.ds(hh * RUN, RUN), :]

    n_e = [0]

    def embed_on(xx, kk, hh, device):
        i = n_e[0]
        n_e[0] += 1
        ref = embed_part(xx, kk, hh)
        send(lambda: copy_to(ref, ref, e_send.at[i], e_recv.at[xx * 4 + kk * 2 + hh], device))

    def embed_arrive(xx, kk, hh):
        ref = embed_part(xx, kk, hh)
        copy_to(ref, ref, e_send.at[0], e_recv.at[xx * 4 + kk * 2 + hh], partner).wait_recv()

    for kk in (k, 1 - k):
        if kk is not k:
            copy_to(own, EB.at[x, kk], v_send.at[0], v_recv.at[1], partner).wait_recv()
        for hh, device in ((0, east), (1, west), (1, east), (0, west)):
            embed_on(x, kk, hh, device)
    for j in range(2):
        for hh in range(2):
            done = ((on00, on01), (on10, on11))[j][hh]
            pl.when(jnp.logical_not(done))(lambda j=j, hh=hh: right_arrive(j, hh))
        left = LB[zl * j]
        theirs = RB[j, pl.ds(pl.multiple_of((1 - k) * HALF, 16), HALF), :]
        PB[j] = lax.dot_general(theirs, left, NT, preferred_element_type=F32).astype(BF)
        send(lambda j=j: copy_to(PB.at[j], QB.at[j], d_send.at[j], d_recv.at[j], partner))
        ours = RB[j, pl.ds(pl.multiple_of(k * HALF, 16), HALF), :]
        SB[j] = lax.dot_general(ours, left, NT, preferred_element_type=F32)

    def quarter(ref, xx):
        return ref.at[pl.ds(pl.multiple_of(xx * FEAT, 8), FEAT), :]

    for j in range(2):
        copy_to(PB.at[j], QB.at[j], d_send.at[j], d_recv.at[j], partner).wait_recv()
        total = SB[j] + QB[j].astype(F32)
        SB[j] = total
        RSF[j] = total.astype(BF)
        for i, dx in enumerate((1, 3, 2)):
            xx = step(x, dx, 4)
            send(
                lambda j=j, i=i, xx=xx: copy_to(
                    quarter(RSF.at[j], xx), RSB.at[j, x], q_send.at[3 * j + i], q_recv.at[4 * j + x],
                    at(xx, y, z, k),
                )
            )

    for kk in (k, 1 - k):
        embed_arrive(xm, kk, 0)
        embed_on(xm, kk, 0, east)
        embed_arrive(xp, kk, 1)
        embed_on(xp, kk, 1, west)

    def result(w, xx):
        return AO.at[w, pl.ds(pl.multiple_of(xx * FEAT, 8), FEAT), :]

    for j in range(2):
        total = SB[j, pl.ds(pl.multiple_of(x * FEAT, 8), FEAT), :]
        for dx in range(1, 4):
            xx = step(x, dx, 4)
            copy_to(RSB.at[j, xx], RSB.at[j, xx], q_send.at[0], q_recv.at[4 * j + xx], partner).wait_recv()
            total += RSB[j, xx].astype(F32)
        w = 2 * zl + j
        AO[w, pl.ds(pl.multiple_of(x * FEAT, 8), FEAT), :] = (RATE * total).astype(BF)
        for i, device in enumerate((pair, east, west)):
            send(
                lambda w=w, i=i, j=j, device=device: copy_to(
                    result(w, x), result(w, x), g_send.at[3 * j + i], g_recv.at[4 * w + x], device
                )
            )

    def result_arrive(w, xx):
        copy_to(result(w, xx), result(w, xx), g_send.at[0], g_recv.at[4 * w + xx], partner).wait_recv()

    for j in range(2):
        w = 2 * (1 - zl) + j
        result_arrive(w, x)
        for i, device in enumerate((east, west)):
            send(
                lambda w=w, i=i, j=j, device=device: copy_to(
                    result(w, x), result(w, x), g_send.at[6 + 2 * j + i], g_recv.at[4 * w + x], device
                )
            )

    def result_part(w, xx, hh):
        return AO.at[w, pl.ds(pl.multiple_of(xx * FEAT + hh * 40, 8), (40, 32)[hh]), :]

    for i, w in enumerate((2 * zl, 2 * zl + 1, 2 * (1 - zl), 2 * (1 - zl) + 1)):
        for hh, xx, device in ((0, xm, east), (1, xp, west)):
            result_arrive(w, xx)
            send(
                lambda w=w, i=i, hh=hh, xx=xx, device=device: copy_to(
                    result_part(w, xx, hh), result_part(w, xx, hh), g_send.at[10 + 2 * i + hh],
                    g_recv.at[16 + 2 * w + hh], device,
                )
            )

    @pl.when(is_router)
    def _():
        for i in range(1, 8):
            ss = step(k * 4 + x, i, 8)
            copy_to(RP.at[ss], RP.at[ss], n_send.at[0], n_recv.at[ss], partner).wait_recv()
        total = jnp.zeros((8, WIDE), F32)
        for ss in range(8):
            total += RP[ss]
        RP[8] = RATE * total

    for dy in range(4):
        for zz in range(2):
            yy, z_to = step(y, dy, 4), 2 * y + zz
            cond = is_router
            if dy == 0 and zz == 0:
                stays = jnp.logical_and(is_router, y == 3)
                local(RP.at[8], router, w_recv.at[0], stays)
                cond = jnp.logical_and(is_router, y != 3)
            send(
                lambda dy=dy, zz=zz, yy=yy, z_to=z_to: copy_to(
                    RP.at[8], router, w_send.at[2 * dy + zz], w_recv.at[0], at(x, yy, z_to, k)
                ),
                cond,
            )

    for kk in (k, 1 - k):
        for xx, hh in ((xm, 1), (xp, 0), (xo, 0), (xo, 1)):
            embed_arrive(xx, kk, hh)
    for w in range(4):
        for hh in range(2):
            ref = result_part(w, xo, hh)
            copy_to(ref, ref, g_send.at[0], g_recv.at[16 + 2 * w + hh], partner).wait_recv()
    pltpu.make_async_copy(router, router, w_recv.at[0]).wait()
    for cond, make in pending:
        if cond is None:
            make().wait_send()
        else:

            @pl.when(cond)
            def _(make=make):
                make().wait_send()


PRE_SEMS = (8, 8, 1, 1, 6, 8, 4, 4, 60, 64, 4, 4, 12, 16, 3, 4, 7, 8)
COMBINE_SEMS = (6, 4, 8, 4, 8, 8, 4, 2, 2, 6, 8, 18, 24, 12, 16, 1, 2, 7, 8, 8, 1)
PRE_BUFFERS = (
    ((24, TOK), F32),
    ((8, 24, TOK), F32),
    ((4, D, TOK), BF),
    ((4, WIDE, WIDE), BF),
    ((4, WIDE, WIDE), F32),
    ((4, WIDE, WIDE), BF),
    ((4, WIDE, WIDE), BF),
    ((4, WIDE, WIDE), BF),
    ((2, 4, WIDE, TOK), BF),
    ((2, WIDE, TOK), F32),
    ((4, 8, 128), F32),
)
COMBINE_BUFFERS = (
    ((2, WIDE, TOK), BF),
    ((2, WIDE, TOK), BF),
    ((WIDE, TOK), BF),
    ((2, HALF, WIDE), BF),
    ((2, HALF, WIDE), BF),
    ((2, HALF, WIDE), F32),
    ((2, HALF, WIDE), BF),
    ((2, 4, FEAT, WIDE), BF),
    ((9, 8, WIDE), F32),
)


def update_kernel(*refs):
    n = len(PRE_BUFFERS) + len(PRE_SEMS)
    operands, (AO, EB, router, all_ids, norms) = refs[:7], refs[7:12]
    lt, rights = refs[12:14]
    settle = precondition_kernel(*operands, lt, rights, all_ids, norms, *refs[14 : 14 + n])
    combine_kernel(lt, rights, AO, EB, router, *refs[14 + n :])
    settle()


def update(*operands):
    return pl.pallas_call(
        update_kernel,
        out_shape=(
            jax.ShapeDtypeStruct((4, HALF, WIDE), BF),
            jax.ShapeDtypeStruct((4, 2, HALF, TOK), BF),
            jax.ShapeDtypeStruct((8, WIDE), F32),
            jax.ShapeDtypeStruct((8, TOK), F32),
            jax.ShapeDtypeStruct((2, FEAT), F32),
        ),
        in_specs=[VM] * 7,
        out_specs=[VM] * 5,
        scratch_shapes=[pltpu.VMEM((WIDE, TOK), BF), pltpu.VMEM((8, TOK), BF)]
        + [pltpu.VMEM(*b) for b in PRE_BUFFERS]
        + [DMA((n,)) for n in PRE_SEMS]
        + [pltpu.VMEM(*b) for b in COMBINE_BUFFERS]
        + [DMA((n,)) for n in COMBINE_SEMS],
        compiler_params=pltpu.CompilerParams(
            collective_id=0, has_side_effects=True, vmem_limit_bytes=60 * 1024 * 1024
        ),
    )(*operands)


STEP = 512


def finish_kernel(AO, EB, router_in, ids, norms_in, diag, attn, embed, router, norms):
    i = pl.program_id(0)
    t = lax.axis_index("tensor")
    attn[...] = AO[...].astype(F32)
    router[...] = router_in[...]
    norms[...] = norms_in[...]
    start = (t * (8192 // 4) + i * STEP).astype(F32)
    vocab = lax.broadcasted_iota(jnp.int32, (STEP, TOK), 0).astype(F32) + start
    total = jnp.zeros((HALF, STEP), F32)
    counts = jnp.zeros((STEP, TOK), F32)
    for xx in range(4):
        for kk in range(2):
            hit = (vocab == ids[kk * 4 + xx : kk * 4 + xx + 1, :]).astype(F32)
            counts += hit
            total += lax.dot_general(EB[xx, kk], hit.astype(BF), NT, preferred_element_type=F32)
    ones = jnp.ones((8, TOK), BF)
    count = lax.dot_general(ones, counts.astype(BF), NT, preferred_element_type=F32)[0:1, :]
    divisor = 0.5 * diag[...] + (0.5 / TOKENS) * count + 0.01
    embed[...] = total * (RATE / divisor)


def finish(AO, EB, router, ids, norms, diag):
    whole = lambda a: pl.BlockSpec(a.shape, lambda i: (0,) * a.ndim)
    return pl.pallas_call(
        finish_kernel,
        grid=(4,),
        out_shape=(
            jax.ShapeDtypeStruct((4, HALF, WIDE), F32),
            jax.ShapeDtypeStruct((HALF, 2048), F32),
            jax.ShapeDtypeStruct((8, WIDE), F32),
            jax.ShapeDtypeStruct((2, FEAT), F32),
        ),
        in_specs=[
            pl.BlockSpec((1, HALF, WIDE), lambda i: (i, 0, 0)),
            whole(EB),
            whole(router),
            whole(ids),
            whole(norms),
            pl.BlockSpec((1, STEP), lambda i: (0, i)),
        ],
        out_specs=[
            pl.BlockSpec((1, HALF, WIDE), lambda i: (i, 0, 0)),
            pl.BlockSpec((HALF, STEP), lambda i: (0, i)),
            pl.BlockSpec((8, WIDE), lambda i: (0, 0)),
            pl.BlockSpec((2, FEAT), lambda i: (0, 0)),
        ],
    )(AO, EB, router, ids, norms, diag)


def per_device(
    activations,
    router_grad,
    token_ids,
    norm_terms,
    old_factors,
    old_router_factor,
    old_norm_diag,
    old_embed_diag,
):
    feats = jnp.transpose(activations, (0, 2, 1))
    old = jnp.transpose(old_factors[0].astype(BF))
    AO, EB, router, ids, norms = update(
        feats, old, router_grad, token_ids[None, :], norm_terms, old_router_factor, old_norm_diag
    )
    attn, embed, router, norms = finish(AO, EB, router, ids, norms, old_embed_diag[None, :])
    return jnp.transpose(attn, (0, 2, 1)), router, norms, jnp.transpose(embed)


def solution(mesh):
    return jax.shard_map(
        per_device,
        mesh=mesh,
        in_specs=(
            P(None, "shard", ("tensor", "section")),
            P(None, "shard"),
            P("shard"),
            P(None, "shard", ("tensor", "section")),
            P("shard", "tensor", "section"),
            P(),
            P(None, ("tensor", "section")),
            P("tensor"),
        ),
        out_specs=(
            P(None, "tensor", "section"),
            P(None, "tensor"),
            P(None, ("tensor", "section")),
            P("tensor", "section"),
        ),
        check_vma=False,
    )
```
